256 devices in a mesh: sub: 32 (over y_lo, z, core), crow: 4 (over x), ccol: 2 (over y_hi).
Axes of the slice: x: 4, y: 4 (y_hi: 2, y_lo: 2; y = y_hi * 2 + y_lo), z: 8, core: 2. Of those that a mesh axis runs over, the one named last changes fastest.
Arguments:
- rhs: float32 [192, 48, 3, 10, 256], P('sub', ('crow', 'ccol')), may hold values from -6 to 6
- start: float32 [192, 48, 3, 10, 256], P('sub', ('crow', 'ccol')), may hold values from -1.75 to 1.75
- stiffness: float32 [192, 48, 3, 10], P('sub', ('crow', 'ccol')), may hold values from 0.1 to 1
- sub_inverse: bfloat16 [256, 1920, 1920], P(('sub', 'crow', 'ccol')), may hold values from -0.0625 to 0.0625
- basis: bfloat16 [256, 1920, 128], P(('sub', 'crow', 'ccol')), may hold values from -0.0625 to 0.0625
- coarse_inverse: bfloat16 [32, 512, 16384], P(None, ('crow', 'ccol'), 'sub'), may hold values from -0.09375 to 0.09375
- offsets: int32 [32, 8], P('sub'), may hold values from 0 to 464, as said below
Outputs:
- solution: float32 [192, 48, 3, 10, 256], P('sub', ('crow', 'ccol'))
The draws below stay inside these ranges and needn't reach their ends.
Inputs may be any that keep to these rules, and one draw needn't show every extreme that they name: In every row g, offsets[g, 0] = 0 and the offsets rise; each count (next offset minus this one, 512 after the last) lies between 48 and 128, and every group has a subdomain with exactly 128.
All inputs are finite; a program needn't handle non-finite values.
Results may differ from the reference program's by a relative error of at most 0.0037.
Values may be sent and summed in bfloat16 or wider, within the bound.
A program may use at most 64 MiB of HBM per device.

```python
import math
import jax
import jax.numpy as jnp
from jax import lax

CS = 6
CQ = 6
CZ = 10
NRHS = 256
ITERS = 2
KMIN = 48
KMEAN = 64
KMAX = 128
GROUP = 8
NLOC = 1920
KGROUP = 512
NCOARSE = 16384
NSUBD = 256
NX = 192
NQ = 48
N_SUB = 32


def draw_offsets(key, part):
    key_big = jax.random.fold_in(key, 11)
    key_cuts = jax.random.fold_in(key, 12)
    spare = GROUP * (KMEAN - KMIN) - (KMAX - KMIN)
    big_member = jax.random.randint(key_big, (N_SUB, 1), 0, GROUP)
    cut_points = jnp.sort(jax.random.randint(key_cuts, (N_SUB, GROUP - 2), 0, spare + 1), axis=1)
    bounds = jnp.concatenate([jnp.zeros((N_SUB, 1), jnp.int32), cut_points.astype(jnp.int32), jnp.full((N_SUB, 1), spare, jnp.int32)], axis=1)
    shares = bounds[:, 1:] - bounds[:, :-1]
    shares_low = jnp.concatenate([shares, jnp.zeros((N_SUB, 1), jnp.int32)], axis=1)
    shares_high = jnp.concatenate([jnp.zeros((N_SUB, 1), jnp.int32), shares], axis=1)
    position = jnp.arange(GROUP, dtype=jnp.int32)[None, :]
    extra = jnp.where(position < big_member, shares_low, jnp.where(position == big_member, KMAX - KMIN, shares_high))
    counts = KMIN + extra
    return (jnp.cumsum(counts, axis=1) - counts).astype(jnp.int32)


def spiked(entries, stream_key, source, target, shards_of, factor):
    owner, partner = [(jnp.arange(entries.shape[dim]) // (entries.shape[dim] // shards_of)).reshape([-1 if axis == dim else 1 for axis in range(entries.ndim)]) for dim in (source, target)]
    chosen = jax.random.permutation(stream_key, shards_of)[partner]
    strong = (owner == chosen) | (owner == (partner + shards_of // 2) % shards_of)
    return jnp.where(strong, factor * entries, entries)


def level_of(rng, shape, split, least, top_value):
    loudness = 1.0
    for dim, blocks in split:
        draws = jax.random.uniform(jax.random.fold_in(jax.random.fold_in(rng, 6), dim), (blocks,), jnp.float32, least / len(split), top_value / len(split))
        loudness = loudness * jnp.repeat(jnp.exp(draws), shape[dim] // blocks).reshape((-1,) + (1,) * (len(shape) - 1 - dim))
    return loudness


def centred(stream_key, extent, deviation, bound, cuts=(), held_as=jnp.bfloat16):
    level = level_of(stream_key, extent, cuts, -0.22, 0.18) if cuts else 1.0
    result = jax.random.normal(stream_key, extent, jnp.float32) * deviation * level
    return jnp.minimum(jnp.maximum(result, -bound), bound).astype(held_as)


def heavy_noise(rng, shape, scale, bound, cuts, heavy, kind=jnp.bfloat16):
    values = scale * jax.random.normal(rng, shape, jnp.float32)
    if cuts:
        values = values * level_of(rng, shape, cuts, -0.22, 0.18)
    return jnp.clip(spiked(values, jax.random.fold_in(rng, 3), *heavy), -bound, bound).astype(kind)


def setup_inputs(seed: int = 0) -> dict:
    seeds = jax.random.split(jax.random.key(seed), 8)
    return {
        "rhs": centred(seeds[0], (NX, NQ, 3, CZ, NRHS), 1.0, 6.0, ((0, 32), (1, 8)), jnp.float32),
        "start": centred(seeds[1], (NX, NQ, 3, CZ, NRHS), 0.3, 1.75, ((0, 32), (1, 8)), jnp.float32),
        "stiffness": jnp.clip(jnp.exp(math.log(1.0) - 2.3025851 * jax.random.uniform(seeds[2], (NX, NQ, 3, CZ), jnp.float32) ** level_of(seeds[2], (NX, NQ, 3, CZ), ((0, 32), (1, 8)), -0.2, 0.2)), 0.1, 1.0),
        "sub_inverse": centred(seeds[3], (NSUBD, NLOC, NLOC), (4 * NLOC) ** -0.5, 0.0625, ((0, 256),)),
        "basis": centred(seeds[4], (NSUBD, NLOC, KMAX), (4 * NLOC) ** -0.5, 0.0625, ((0, 256),)),
        "coarse_inverse": heavy_noise(seeds[5], (N_SUB, KGROUP, NCOARSE), NCOARSE ** -0.5, 0.09375, ((1, 8), (2, 32)), (2, 0, 32, 2.75)),
        "offsets": draw_offsets(jax.random.fold_in(seeds[7], 71), 0),
    }


def apply_stiffness(field, stiffness):
    padded = jnp.pad(field, ((1, 1), (1, 1), (0, 0), (1, 1), (0, 0)))
    beside = padded[2:, 1:-1, :, 1:-1] + padded[:-2, 1:-1, :, 1:-1]
    beside = beside + padded[1:-1, 2:, :, 1:-1] + padded[1:-1, :-2, :, 1:-1]
    beside = beside + padded[1:-1, 1:-1, :, 2:] + padded[1:-1, 1:-1, :, :-2]
    return (6.0 + stiffness)[..., None] * field - beside


def window(padded_res, domain):
    group_id = (domain // GROUP).astype(jnp.int32)
    member_id = (domain % GROUP).astype(jnp.int32)
    zero = jnp.zeros((), jnp.int32)
    corner_s = (group_id * CS).astype(jnp.int32)
    corner_q = (member_id * CQ).astype(jnp.int32)
    piece = lax.dynamic_slice(padded_res, (corner_s, corner_q, zero, zero, zero), (CS + 2, CQ + 2, 3, CZ, NRHS))
    return piece.reshape(NLOC, NRHS)


def selector_for(offsets, counts, domain):
    group_id = domain // GROUP
    member_id = domain % GROUP
    first_slot = offsets[group_id, member_id]
    col_count = counts[group_id, member_id]
    slot_ids = jnp.arange(KGROUP, dtype=jnp.int32)[:, None]
    col_ids = jnp.arange(KMAX, dtype=jnp.int32)[None, :]
    selector = ((slot_ids == first_slot + col_ids) & (col_ids < col_count)).astype(jnp.bfloat16)
    return selector, col_count


def reference(rhs, start, stiffness, sub_inverse, basis, coarse_inverse, offsets):
    counts = jnp.concatenate([offsets[:, 1:], jnp.full((N_SUB, 1), KGROUP, jnp.int32)], axis=1) - offsets
    domains = jnp.arange(N_SUB * GROUP, dtype=jnp.int32)
    solution = start
    for sweep in range(ITERS):
        residual = rhs - apply_stiffness(solution, stiffness)
        padded_res = jnp.pad(residual, ((1, 1), (1, 1), (0, 0), (0, 0), (0, 0))).astype(jnp.bfloat16)

        def restrict(domain):
            local_res = window(padded_res, domain)
            selector, col_count = selector_for(offsets, counts, domain)
            own_basis = lax.dynamic_index_in_dim(basis, domain, 0, keepdims=False)
            projected = jnp.dot(own_basis.T, local_res, preferred_element_type=jnp.float32)
            keep = jnp.arange(KMAX, dtype=jnp.int32)[:, None] < col_count
            restricted = jnp.where(keep, projected, jnp.zeros_like(projected)).astype(jnp.bfloat16)
            return jnp.dot(selector, restricted, preferred_element_type=jnp.float32)

        placed = lax.map(restrict, domains)
        coefficients = placed.reshape(N_SUB, GROUP, KGROUP, NRHS).sum(axis=1).astype(jnp.bfloat16)
        flat_coeffs = coefficients.reshape(N_SUB * KGROUP, NRHS)

        def coarse_rows(group_rows):
            return jnp.dot(group_rows, flat_coeffs, preferred_element_type=jnp.float32)

        row_values = lax.map(coarse_rows, coarse_inverse).astype(jnp.bfloat16)
        coarse_values = row_values.reshape(N_SUB, GROUP, KMEAN, NRHS).transpose(0, 2, 1, 3).reshape(N_SUB, KGROUP, NRHS)

        def correct(domain):
            local_res = window(padded_res, domain)
            selector, col_count = selector_for(offsets, counts, domain)
            own_basis = lax.dynamic_index_in_dim(basis, domain, 0, keepdims=False)
            own_inverse = lax.dynamic_index_in_dim(sub_inverse, domain, 0, keepdims=False)
            own_values = lax.dynamic_index_in_dim(coarse_values, domain // GROUP, 0, keepdims=False)
            selected = jnp.dot(selector.T, own_values, preferred_element_type=jnp.float32).astype(jnp.bfloat16)
            fine_part = jnp.dot(own_inverse, local_res, preferred_element_type=jnp.float32)
            coarse_part = jnp.dot(own_basis, selected, preferred_element_type=jnp.float32)
            total = (fine_part + coarse_part).reshape(CS + 2, CQ + 2, 3, CZ, NRHS)
            return total[1:-1, 1:-1]

        pieces = lax.map(correct, domains)
        correction = pieces.reshape(N_SUB, GROUP, CS, CQ, 3, CZ, NRHS).transpose(0, 2, 1, 3, 4, 5, 6)
        correction = correction.reshape(N_SUB * CS, GROUP * CQ, 3, CZ, NRHS)
        solution = solution + correction
    return solution
```

```python
import functools

import jax
import jax.numpy as jnp
from jax import lax
from jax.experimental import pallas as pl
from jax.experimental.pallas import tpu as pltpu
from jax.sharding import PartitionSpec as P

MESH = pl.DeviceIdType.MESH
SWEEPS = 2
SIDE = 6
EXT = 8
ROWS = 30
CELL = 32
SLAB = EXT * ROWS
PADSLAB = EXT * CELL
INNER = SIDE * CELL
NLOC = EXT * SLAB
LANES = 256
MEMBERS = 8
KMAX = 128
KGROUP = 512
SHARE = 64
NZ = 8
ZORDER = (4, 3, 5, 2, 6, 1, 7, 0)
F32 = jnp.float32
BF16 = jnp.bfloat16


def iota(shape, dim):
    return lax.broadcasted_iota(jnp.int32, shape, dim)


def one_hot(mask):
    return jnp.where(mask, 1.0, 0.0).astype(BF16)


def dot(a, b):
    return jnp.dot(a, b, preferred_element_type=F32)


def kernel(
    nch,
    offs,
    start_hbm,
    rhs,
    diag,
    w_hbm,
    basis_hbm,
    c_hbm,
    out,
    uext,
    res,
    loc,
    locc,
    wraw,
    wp,
    braw,
    bint,
    bt,
    cbuf,
    place,
    pick,
    fine,
    pb,
    hsend,
    hrecv,
    csend_corner,
    crecv_corner,
    pieces,
    cores,
    corer,
    ysend,
    yrecv,
    zsend,
    zrecv,
    cvals,
    load_sem,
    halo_s,
    halo_r,
    g1_s,
    g1_r,
    core_s,
    core_r,
    y_s,
    y_r,
    z_s,
    z_r,
    g2_s,
    g2_r,
):
    width = LANES // nch
    g = lax.axis_index("sub")
    crow = lax.axis_index("crow")
    ccol = lax.axis_index("ccol")
    m = crow * 2 + ccol
    core = lax.rem(g, 2)
    z = lax.rem(g // 2, NZ)
    ylo = g // (2 * NZ)

    def at(gg, mm):
        return (gg, mm // 2, lax.rem(mm, 2))

    def sub_of(yy, zz, cc):
        return (yy * NZ + zz) * 2 + cc

    gp, gm = lax.rem(g + 1, 32), lax.rem(g + 31, 32)
    mp, mm = lax.rem(m + 1, MEMBERS), lax.rem(m + 7, MEMBERS)
    halo_to = [
        at(gp, m), at(gm, m), at(g, mp), at(g, mm),
        at(gp, mp), at(gp, mm), at(gm, mp), at(gm, mm),
    ]
    group_to = [at(g, lax.rem(m + j, MEMBERS)) for j in range(MEMBERS)]
    core_to = at(sub_of(ylo, z, 1 - core), m)
    y_to = at(sub_of(1 - ylo, z, core), m)
    z_to = [at(sub_of(ylo, lax.rem(z + k, NZ), core), m) for k in range(NZ)]
    partners = halo_to + group_to[1:] + [core_to, y_to] + z_to[1:]

    barrier = pltpu.get_barrier_semaphore()
    for device in partners:
        pl.semaphore_signal(barrier, inc=1, device_id=device, device_id_type=MESH)

    loads = [
        pltpu.make_async_copy(
            start_hbm, uext.at[pl.ds(1, SIDE), pl.ds(1, SIDE)], load_sem.at[0]
        ),
        pltpu.make_async_copy(basis_hbm, braw, load_sem.at[1]),
        pltpu.make_async_copy(c_hbm.at[:, 0], cbuf.at[0], load_sem.at[2]),
        pltpu.make_async_copy(c_hbm.at[:, 1], cbuf.at[1], load_sem.at[3]),
    ] + [
        pltpu.make_async_copy(
            w_hbm.at[pl.ds((s + 1) * SLAB + 24, INNER)], wraw.at[s], load_sem.at[4 + s]
        )
        for s in range(SIDE)
    ]
    for copy in loads:
        copy.start()

    zero_row = jnp.zeros((EXT, CELL, LANES), F32)
    uext[0] = zero_row
    uext[EXT - 1] = zero_row
    for s in range(1, EXT - 1):
        uext[s, 0] = zero_row[0]
        uext[s, EXT - 1] = zero_row[0]

    row = iota((CELL, 128), 0)
    layer = lax.rem(row, 10)
    has_below = layer != 0
    has_above = jnp.logical_and(layer != 9, row < ROWS)
    ok_sm, ok_sp, ok_qm, ok_qp = g > 0, g < 31, m > 0, m < MEMBERS - 1

    def remote(src, dst, send, recv, device):
        return pltpu.make_async_remote_copy(
            src_ref=src,
            dst_ref=dst,
            send_sem=send,
            recv_sem=recv,
            device_id=device,
            device_id_type=MESH,
        )

    def halo_copies(t, c):
        out_copies = []
        for d in range(4):
            out_copies.append(
                remote(
                    hsend.at[t, c, d], hrecv.at[t, c, d],
                    halo_s.at[t, c, d], halo_r.at[t, c, d], halo_to[d],
                )
            )
        for d in range(4):
            out_copies.append(
                remote(
                    csend_corner.at[t, c, d], crecv_corner.at[t, c, d],
                    halo_s.at[t, c, 4 + d], halo_r.at[t, c, 4 + d], halo_to[4 + d],
                )
            )
        return out_copies

    def lane_tiles(c):
        return [(c * width + i * 128, i * 128) for i in range(width // 128)]

    def stencil(t, c):
        base = rhs if t == 0 else res

        def step(s, carry):
            for lane, _ in lane_tiles(c):
                ls = pl.ds(lane, 128)
                for q in range(SIDE):
                    u = uext[s + 1, q + 1, :, ls]
                    beside = (
                        uext[s, q + 1, :, ls] + uext[s + 2, q + 1, :, ls]
                        + uext[s + 1, q, :, ls] + uext[s + 1, q + 2, :, ls]
                    )
                    beside = beside + jnp.where(has_below, pltpu.roll(u, 1, 0), 0.0)
                    beside = beside + jnp.where(has_above, pltpu.roll(u, CELL - 1, 0), 0.0)
                    res[s, q, :, ls] = base[s, q, :, ls] - (diag[s, q] * u - beside)
            return carry

        lax.fori_loop(0, SIDE, step, 0)
        for lane, dst in lane_tiles(c):
            ls, ds = pl.ds(lane, 128), pl.ds(dst, 128)
            for i in range(SIDE):
                for d, (s, q) in enumerate(((SIDE - 1, i), (0, i), (i, SIDE - 1), (i, 0))):
                    hsend[t, c, d, 0, i, :, ds] = uext[s + 1, q + 1, :, ls].astype(BF16)
                    hsend[t, c, d, 1, i, :, ds] = res[s, q, :, ls].astype(BF16)
            for d, (s, q) in enumerate(((5, 5), (5, 0), (0, 5), (0, 0))):
                csend_corner[t, c, d, 0, :, ds] = uext[s + 1, q + 1, :, ls].astype(BF16)
                csend_corner[t, c, d, 1, :, ds] = res[s, q, :, ls].astype(BF16)

    def finish_residual(t, c):
        for lane, dst in lane_tiles(c):
            ls, ds = pl.ds(lane, 128), pl.ds(dst, 128)

            def got(d, field, i, ok):
                return jnp.where(ok, hrecv[t, c, d, field, i, :, ds].astype(F32), 0.0)

            def corner(d, field, ok):
                return jnp.where(ok, crecv_corner[t, c, d, field, :, ds].astype(F32), 0.0)

            oks = (ok_sm, ok_sp, ok_qm, ok_qp)
            diag_ok = (
                jnp.logical_and(ok_sm, ok_qm), jnp.logical_and(ok_sm, ok_qp),
                jnp.logical_and(ok_sp, ok_qm), jnp.logical_and(ok_sp, ok_qp),
            )
            cu = [corner(d, 0, diag_ok[d]) for d in range(4)]
            for s in range(SIDE):
                for q in range(SIDE):
                    value = res[s, q, :, ls]
                    edge = False
                    for d, here, i in ((0, s == 0, q), (1, s == 5, q), (2, q == 0, s), (3, q == 5, s)):
                        if here:
                            value = value + got(d, 0, i, oks[d])
                            edge = True
                    if edge:
                        res[s, q, :, ls] = value
                    loc[s + 1, q + 1, :, ls] = value.astype(BF16)
            for d in range(4):
                for i in range(SIDE):
                    s, q = ((0, i), (5, i), (i, 0), (i, 5))[d]
                    value = hrecv[t, c, d, 1, i, :, ds].astype(F32) + uext[s + 1, q + 1, :, ls]
                    if i == 0:
                        value = value + cu[(0, 2, 0, 1)[d]]
                    if i == SIDE - 1:
                        value = value + cu[(1, 3, 2, 3)[d]]
                    value = jnp.where(oks[d], value, 0.0).astype(BF16)
                    s, q = ((0, i + 1), (7, i + 1), (i + 1, 0), (i + 1, 7))[d]
                    loc[s, q, :, ls] = value
            for d in range(4):
                sd, qd = ((0, 2), (0, 3), (1, 2), (1, 3))[d]
                si, qi = ((0, 0), (5, 0), (0, 5), (5, 5))[d]
                value = crecv_corner[t, c, d, 1, :, ds].astype(F32)
                value = value + hrecv[t, c, sd, 0, si, :, ds].astype(F32)
                value = value + hrecv[t, c, qd, 0, qi, :, ds].astype(F32)
                value = jnp.where(diag_ok[d], value, 0.0).astype(BF16)
                s, q = ((0, 0), (0, 7), (7, 0), (7, 7))[d]
                loc[s, q, :, ls] = value

    own_offset = offs[m]
    own_count = jnp.where(m == MEMBERS - 1, KGROUP, offs[jnp.minimum(m + 1, MEMBERS - 1)]) - own_offset

    def tables():
        slot = iota((KGROUP, KMAX), 0)
        k = iota((KGROUP, KMAX), 1)
        for j in range(MEMBERS):
            first = offs[j]
            limit = (KGROUP if j == MEMBERS - 1 else offs[j + 1]) - first
            place[:, j * KMAX:(j + 1) * KMAX] = one_hot(
                jnp.logical_and(slot == first + k, k < limit)
            )
        k = iota((KMAX, KGROUP), 0)
        index = iota((KMAX, KGROUP), 1)
        slot = (index % SHARE) * MEMBERS + index // SHARE
        pick[...] = one_hot(jnp.logical_and(slot == own_offset + k, k < own_count))

    def expand_basis():
        j, i = iota((PADSLAB, SLAB), 0), iota((PADSLAB, SLAB), 1)
        spread = one_hot(
            jnp.logical_and(i == (j // CELL) * ROWS + j % CELL, j % CELL < ROWS)
        )
        for s in range(EXT):
            part = dot(spread, braw[s * SLAB:(s + 1) * SLAB, :])
            bt[:, s * PADSLAB:(s + 1) * PADSLAB] = part.T.astype(BF16)
            if 1 <= s <= SIDE:
                bint[(s - 1) * INNER:s * INNER, :] = part[CELL:CELL + INNER, :].astype(BF16)

    def expand_inverse():
        j, i = iota((INNER, INNER), 0), iota((INNER, INNER), 1)
        spread = one_hot(
            jnp.logical_and(i == 6 + (j // CELL) * ROWS + j % CELL, j % CELL < ROWS)
        )

        def step(s, carry):
            wp[pl.ds(pl.multiple_of(s * INNER, INNER), INNER), :] = dot(
                spread, wraw[s]
            ).astype(BF16)
            return carry

        lax.fori_loop(0, SIDE, step, 0)

    def gather_one(t, c):
        return [
            remote(
                pieces.at[t, c, m], pieces.at[t, c, m],
                g1_s.at[t, c, j], g1_r.at[t, c, j], group_to[j],
            )
            for j in range(1, MEMBERS)
        ]

    def gather_two(t, c):
        return [
            remote(
                cvals.at[t, c, m], cvals.at[t, c, m],
                g2_s.at[t, c, j], g2_r.at[t, c, j], group_to[j],
            )
            for j in range(1, MEMBERS)
        ]

    def restrict(t, c):
        ls = pl.ds(c * width, width)
        local = loc[:, :, :, ls].reshape(EXT * PADSLAB, width)
        projected = dot(bt[...], local)
        keep = iota((KMAX, width), 0) < own_count
        pieces[t, c, m] = jnp.where(keep, projected, 0.0).astype(BF16)

    def fine_product(c):
        ls = pl.ds(c * width, width)
        i, j = iota((SLAB, PADSLAB), 0), iota((SLAB, PADSLAB), 1)
        pack = one_hot(
            jnp.logical_and(i == (j // CELL) * ROWS + j % CELL, j % CELL < ROWS)
        )
        for s in range(EXT):
            locc[s * SLAB:(s + 1) * SLAB, ls] = dot(
                pack, loc[s, :, :, ls].reshape(PADSLAB, width)
            ).astype(BF16)
        fine[:, ls] = dot(wp[...], locc[:, ls])

    def core_copies(t, c):
        return [
            remote(
                cores.at[t, c, h], corer.at[t, c, h],
                core_s.at[t, c, h], core_r.at[t, c, h], core_to,
            )
            for h in range(2)
        ]

    def y_copies(t, c):
        return [
            remote(
                ysend.at[t, c, k], yrecv.at[t, c, k],
                y_s.at[t, c, k], y_r.at[t, c, k], y_to,
            )
            for k in range(NZ)
        ]

    def z_copies(t, c):
        return [
            remote(
                zsend.at[t, c, k], zrecv.at[t, c, k],
                z_s.at[t, c, k], z_r.at[t, c, k], z_to[k],
            )
            for k in range(NZ)
        ]

    def coarse(t, c):
        coef = dot(place[...], pieces[t, c].reshape(MEMBERS * KMAX, width)).astype(BF16)
        copies = core_copies(t, c)
        for h, half in ((0, 1 - ylo), (1, ylo)):
            rows = cbuf[1 - core, pl.ds(half * NZ, NZ)].reshape(NZ * SHARE, KGROUP)
            cores[t, c, h] = dot(rows, coef).astype(BF16).reshape(NZ, SHARE, width)
            copies[h].start()
        for h, half in ((0, 1 - ylo), (1, ylo)):
            rows = cbuf[core, pl.ds(half * NZ, NZ)].reshape(NZ * SHARE, KGROUP)
            pb[c, h] = dot(rows, coef).reshape(NZ, SHARE, width)

    def reduce_sums(t, c):
        copies, ys, zs = core_copies(t, c), y_copies(t, c), z_copies(t, c)
        copies[0].wait_recv()
        for k in ZORDER:
            zz = lax.rem(z + k, NZ)
            ysend[t, c, k] = (pb[c, 0, zz] + corer[t, c, 0, zz].astype(F32)).astype(BF16)
            ys[k].start()
        copies[1].wait_recv()
        for k in ZORDER:
            zz = lax.rem(z + k, NZ)
            ys[k].wait_recv()
            value = pb[c, 1, zz] + corer[t, c, 1, zz].astype(F32) + yrecv[t, c, k].astype(F32)
            if k == 0:
                total = value
            else:
                zsend[t, c, k] = value.astype(BF16)
                zs[k].start()
        for k in ZORDER[::-1]:
            if k:
                zs[k].wait_recv()
                total = total + zrecv[t, c, k].astype(F32)
        cvals[t, c, m] = total.astype(BF16)

    def correct(t, c):
        ls = pl.ds(c * width, width)
        chosen = dot(pick[...], cvals[t, c].reshape(MEMBERS * SHARE, width)).astype(BF16)
        for s in range(SIDE):
            rows = slice(s * INNER, (s + 1) * INNER)
            total = fine[rows, ls] + dot(bint[rows, :], chosen)
            total = total.reshape(SIDE, CELL, width)
            if t == 0:
                out[s, :, :, ls] = uext[s + 1, 1:1 + SIDE, :, ls] + total
                uext[s + 1, 1:1 + SIDE, :, ls] = total
            else:
                out[s, :, :, ls] = out[s, :, :, ls] + total

    def start_all(copies):
        for copy in copies:
            copy.start()

    def recv_all(copies):
        for copy in copies:
            copy.wait_recv()

    chunks = range(nch)
    loads[0].wait()
    for c in chunks:
        stencil(0, c)
    pl.semaphore_wait(barrier, len(partners))
    for t in range(SWEEPS):
        for c in chunks:
            if t:
                stencil(t, c)
            start_all(halo_copies(t, c))
        if t == 0:
            tables()
            loads[1].wait()
            expand_basis()
        for c in chunks:
            recv_all(halo_copies(t, c))
            finish_residual(t, c)
            restrict(t, c)
            start_all(gather_one(t, c))
        if t == 0:
            for copy in loads[2:]:
                copy.wait()
            expand_inverse()
        for c in chunks:
            fine_product(c)
        for c in chunks:
            recv_all(gather_one(t, c))
            coarse(t, c)
        for c in chunks:
            reduce_sums(t, c)
            start_all(gather_two(t, c))
        for c in chunks:
            recv_all(gather_two(t, c))
            correct(t, c)
    for t in range(SWEEPS):
        for c in chunks:
            for copy in (
                halo_copies(t, c) + gather_one(t, c) + core_copies(t, c)
                + y_copies(t, c) + z_copies(t, c)[1:] + gather_two(t, c)
            ):
                copy.wait_send()


def shards(nch, rhs, start, stiffness, sub_inverse, basis, coarse_inverse, offsets):
    def cells(field):
        flat = field.reshape(SIDE, SIDE, ROWS, LANES)
        return jnp.pad(flat, ((0, 0), (0, 0), (0, CELL - ROWS), (0, 0)))

    diag = (6.0 + stiffness).reshape(SIDE, SIDE, ROWS)
    diag = jnp.pad(diag, ((0, 0), (0, 0), (0, CELL - ROWS)))
    diag = jnp.broadcast_to(diag[..., None], (SIDE, SIDE, CELL, 128))
    width = LANES // nch
    lead = (SWEEPS, nch)
    vmem = pl.BlockSpec(memory_space=pltpu.VMEM)
    hbm = pl.BlockSpec(memory_space=pl.ANY)
    dma = pltpu.SemaphoreType.DMA
    out = pl.pallas_call(
        functools.partial(kernel, nch),
        name="schwarz",
        out_shape=jax.ShapeDtypeStruct((SIDE, SIDE, CELL, LANES), F32),
        in_specs=[pl.BlockSpec(memory_space=pltpu.SMEM), hbm, vmem, vmem, hbm, hbm, hbm],
        out_specs=vmem,
        scratch_shapes=[
            pltpu.VMEM((EXT, EXT, CELL, LANES), F32),
            pltpu.VMEM((SIDE, SIDE, CELL, LANES), F32),
            pltpu.VMEM((EXT, EXT, CELL, LANES), BF16),
            pltpu.VMEM((NLOC, LANES), BF16),
            pltpu.VMEM((SIDE, INNER, NLOC), BF16),
            pltpu.VMEM((SIDE * INNER, NLOC), BF16),
            pltpu.VMEM((NLOC, KMAX), BF16),
            pltpu.VMEM((SIDE * INNER, KMAX), BF16),
            pltpu.VMEM((KMAX, EXT * PADSLAB), BF16),
            pltpu.VMEM((2, 2 * NZ, SHARE, KGROUP), BF16),
            pltpu.VMEM((KGROUP, MEMBERS * KMAX), BF16),
            pltpu.VMEM((KMAX, KGROUP), BF16),
            pltpu.VMEM((SIDE * INNER, LANES), F32),
            pltpu.VMEM((nch, 2, NZ, SHARE, width), F32),
            pltpu.VMEM(lead + (4, 2, SIDE, CELL, width), BF16),
            pltpu.VMEM(lead + (4, 2, SIDE, CELL, width), BF16),
            pltpu.VMEM(lead + (4, 2, CELL, width), BF16),
            pltpu.VMEM(lead + (4, 2, CELL, width), BF16),
            pltpu.VMEM(lead + (MEMBERS, KMAX, width), BF16),
            pltpu.VMEM(lead + (2, NZ, SHARE, width), BF16),
            pltpu.VMEM(lead + (2, NZ, SHARE, width), BF16),
            pltpu.VMEM(lead + (NZ, SHARE, width), BF16),
            pltpu.VMEM(lead + (NZ, SHARE, width), BF16),
            pltpu.VMEM(lead + (NZ, SHARE, width), BF16),
            pltpu.VMEM(lead + (NZ, SHARE, width), BF16),
            pltpu.VMEM(lead + (MEMBERS, SHARE, width), BF16),
            dma((4 + SIDE,)),
            dma(lead + (8,)), dma(lead + (8,)),
            dma(lead + (8,)), dma(lead + (8,)),
            dma(lead + (2,)), dma(lead + (2,)),
            dma(lead + (8,)), dma(lead + (8,)),
            dma(lead + (8,)), dma(lead + (8,)),
            dma(lead + (8,)), dma(lead + (8,)),
        ],
        compiler_params=pltpu.CompilerParams(
            collective_id=0, has_side_effects=True, vmem_limit_bytes=56 * 1024 * 1024
        ),
    )(
        offsets[0],
        cells(start),
        cells(rhs),
        diag,
        sub_inverse[0],
        basis[0],
        coarse_inverse.reshape(2 * NZ, 2, SHARE, KGROUP),
    )
    return out[:, :, :ROWS, :].reshape(rhs.shape)


def solution(mesh):
    return jax.shard_map(
        functools.partial(shards, 1),
        mesh=mesh,
        in_specs=(
            P("sub", ("crow", "ccol"), None, None, None),
            P("sub", ("crow", "ccol"), None, None, None),
            P("sub", ("crow", "ccol"), None, None),
            P(("sub", "crow", "ccol"), None, None),
            P(("sub", "crow", "ccol"), None, None),
            P(None, ("crow", "ccol"), "sub"),
            P("sub", None),
        ),
        out_specs=P("sub", ("crow", "ccol"), None, None, None),
        check_vma=False,
    )
```

```python
import functools

import jax
import jax.numpy as jnp
from jax import lax
from jax.experimental import pallas as pl
from jax.experimental.pallas import tpu as pltpu
from jax.sharding import PartitionSpec as P

MESH = pl.DeviceIdType.MESH
SWEEPS = 2
SIDE = 6
EXT = 8
ROWS = 30
CELL = 32
SLAB = EXT * ROWS
PADSLAB = EXT * CELL
INNER = SIDE * CELL
NLOC = EXT * SLAB
LANES = 256
MEMBERS = 8
KMAX = 128
KGROUP = 512
SHARE = 64
NZ = 8
ZORDER = (4, 3, 5, 2, 6, 1, 7, 0)
SPOT = (0, 2, 3, 4, 5, 1)
GORDER = (5, 3, 7, 1, 4, 2, 6)
F32 = jnp.float32
BF16 = jnp.bfloat16


def iota(shape, dim):
    return lax.broadcasted_iota(jnp.int32, shape, dim)


def one_hot(mask):
    return jnp.where(mask, 1.0, 0.0).astype(BF16)


def dot(a, b):
    return jnp.dot(a, b, preferred_element_type=F32)


def kernel(
    nch,
    offs,
    start_hbm,
    rhs_hbm,
    stiff,
    w_hbm,
    basis_hbm,
    c_hbm,
    out,
    start_raw,
    rhs_raw,
    diag,
    sol,
    uext,
    res,
    loc,
    locc,
    wraw,
    wp,
    braw,
    bint,
    bt,
    cbuf,
    coef,
    place,
    pick,
    fine,
    pb,
    hsend,
    hrecv,
    corners,
    pieces,
    cores,
    corer,
    ysend,
    yrecv,
    zsend,
    zrecv,
    cvals,
    load_sem,
    halo_s,
    halo_r,
    corner_s,
    corner_r,
    g1_s,
    g1_r,
    core_s,
    core_r,
    y_s,
    y_r,
    z_s,
    z_r,
    g2_s,
    g2_r,
):
    width = LANES // nch
    g = lax.axis_index("sub")
    crow = lax.axis_index("crow")
    ccol = lax.axis_index("ccol")
    m = crow * 2 + ccol
    core = lax.rem(g, 2)
    z = lax.rem(g // 2, NZ)
    ylo = g // (2 * NZ)

    def at(gg, mm):
        return (gg, mm // 2, lax.rem(mm, 2))

    def sub_of(yy, zz, cc):
        return (yy * NZ + zz) * 2 + cc

    gp, gm = lax.rem(g + 1, 32), lax.rem(g + 31, 32)
    mp, mm = lax.rem(m + 1, MEMBERS), lax.rem(m + 7, MEMBERS)
    halo_to = [at(gp, m), at(gm, m), at(g, mp), at(g, mm)]
    group_to = [at(g, lax.rem(m + j, MEMBERS)) for j in range(MEMBERS)]
    core_to = at(sub_of(ylo, z, 1 - core), m)
    y_to = at(sub_of(1 - ylo, z, core), m)
    z_to = [at(sub_of(ylo, lax.rem(z + k, NZ), core), m) for k in range(NZ)]
    partners = halo_to + group_to[1:] + [core_to, y_to] + z_to[1:]

    barrier = pltpu.get_barrier_semaphore()
    for device in partners:
        pl.semaphore_signal(barrier, inc=1, device_id=device, device_id_type=MESH)

    loads = [
        pltpu.make_async_copy(start_hbm, start_raw, load_sem.at[0]),
        pltpu.make_async_copy(rhs_hbm, rhs_raw, load_sem.at[4 + SIDE]),
        pltpu.make_async_copy(basis_hbm, braw, load_sem.at[1]),
        pltpu.make_async_copy(c_hbm.at[:, 0], cbuf.at[0], load_sem.at[2]),
        pltpu.make_async_copy(c_hbm.at[:, 1], cbuf.at[1], load_sem.at[3]),
    ] + [
        pltpu.make_async_copy(
            w_hbm.at[pl.ds((s + 1) * SLAB + 24, INNER)], wraw.at[s], load_sem.at[4 + s]
        )
        for s in range(SIDE)
    ]
    for copy in loads:
        copy.start()

    zero_row = jnp.zeros((EXT, CELL, LANES), F32)
    uext[0] = zero_row
    uext[EXT - 1] = zero_row
    for s in range(1, EXT - 1):
        uext[s, 0] = zero_row[0]
        uext[s, EXT - 1] = zero_row[0]
        uext[s, 1:EXT - 1, 24:CELL, :] = jnp.zeros((SIDE, CELL - 24, LANES), F32)

    row = iota((CELL, 128), 0)
    layer = lax.rem(row, 10)
    has_below = layer != 0
    has_above = jnp.logical_and(layer != 9, row < ROWS)
    ok_sm, ok_sp, ok_qm, ok_qp = g > 0, g < 31, m > 0, m < MEMBERS - 1

    def remote(src, dst, send, recv, device):
        return pltpu.make_async_remote_copy(
            src_ref=src,
            dst_ref=dst,
            send_sem=send,
            recv_sem=recv,
            device_id=device,
            device_id_type=MESH,
        )

    def halo_copies(t, c, part, sides):
        where = pl.ds(0, 2) if part == 0 else pl.ds(2, 4)
        return [
            remote(
                hsend.at[t, c, d, :, where], hrecv.at[t, c, d, :, where],
                halo_s.at[t, c, part, d], halo_r.at[t, c, part, d], halo_to[d],
            )
            for d in sides
        ]

    def corner_copies(t, c):
        return [
            remote(
                hrecv.at[t, c, side, :, end], corners.at[t, c, d],
                corner_s.at[t, c, d], corner_r.at[t, c, d], halo_to[to],
            )
            for d, side, end, to in ((0, 2, 1, 0), (1, 3, 1, 0), (2, 2, 0, 1), (3, 3, 0, 1))
        ]

    def unpack_inputs():
        first = lax.rem(iota((CELL, 10), 0), 10) == iota((CELL, 10), 1)
        comp = iota((CELL, 10), 0) // 10

        def step(s, carry):
            for q in range(SIDE):
                k = stiff[s, q]
                spread = jnp.where(comp == 0, k[0:1], jnp.where(comp == 1, k[1:2], k[2:3]))
                column = jnp.sum(jnp.where(first, spread, 0.0), axis=1, keepdims=True)
                diag[s, q] = jnp.broadcast_to(6.0 + column, (CELL, 128))
                for lane in range(0, LANES, 128):
                    ls = pl.ds(lane, 128)
                    res[s, q, pl.ds(24, 8), ls] = jnp.zeros((8, 128), F32)
                    for comp_id in range(3):
                        rows = pl.ds(comp_id * 10, 10)
                        uext[s + 1, q + 1, rows, ls] = start_raw[s, q, :, comp_id, ls]
                        res[s, q, rows, ls] = rhs_raw[s, q, :, comp_id, ls]
            return carry

        lax.fori_loop(0, SIDE, step, 0)

    def lane_tiles(c):
        return [(c * width + i * 128, i * 128) for i in range(width // 128)]

    def stencil(t, c):
        def step(s, carry):
            for lane, _ in lane_tiles(c):
                ls = pl.ds(lane, 128)
                for q in range(SIDE):
                    u = uext[s + 1, q + 1, :, ls]
                    beside = (
                        uext[s, q + 1, :, ls] + uext[s + 2, q + 1, :, ls]
                        + uext[s + 1, q, :, ls] + uext[s + 1, q + 2, :, ls]
                    )
                    beside = beside + jnp.where(has_below, pltpu.roll(u, 1, 0), 0.0)
                    beside = beside + jnp.where(has_above, pltpu.roll(u, CELL - 1, 0), 0.0)
                    res[s, q, :, ls] = res[s, q, :, ls] - (diag[s, q] * u - beside)
            return carry

        lax.fori_loop(0, SIDE, step, 0)
        for lane, dst in lane_tiles(c):
            ls, ds = pl.ds(lane, 128), pl.ds(dst, 128)
            for i in range(SIDE):
                for d, (s, q) in enumerate(((SIDE - 1, i), (0, i), (i, SIDE - 1), (i, 0))):
                    hsend[t, c, d, 0, SPOT[i], :, ds] = uext[s + 1, q + 1, :, ls].astype(BF16)
                    hsend[t, c, d, 1, SPOT[i], :, ds] = res[s, q, :, ls].astype(BF16)

    def finish_residual(t, c):
        for lane, dst in lane_tiles(c):
            ls, ds = pl.ds(lane, 128), pl.ds(dst, 128)

            def got(d, field, i, ok):
                return jnp.where(ok, hrecv[t, c, d, field, SPOT[i], :, ds].astype(F32), 0.0)

            def corner(d, field, ok):
                return jnp.where(ok, corners[t, c, d, field, :, ds].astype(F32), 0.0)

            oks = (ok_sm, ok_sp, ok_qm, ok_qp)
            diag_ok = (
                jnp.logical_and(ok_sm, ok_qm), jnp.logical_and(ok_sm, ok_qp),
                jnp.logical_and(ok_sp, ok_qm), jnp.logical_and(ok_sp, ok_qp),
            )
            cu = [corner(d, 0, diag_ok[d]) for d in range(4)]
            for s in range(SIDE):
                for q in range(SIDE):
                    value = res[s, q, :, ls]
                    edge = False
                    for d, here, i in ((0, s == 0, q), (1, s == 5, q), (2, q == 0, s), (3, q == 5, s)):
                        if here:
                            value = value + got(d, 0, i, oks[d])
                            edge = True
                    if edge:
                        res[s, q, :, ls] = value
                    loc[s + 1, q + 1, :, ls] = value.astype(BF16)
            for d in range(4):
                for i in range(SIDE):
                    s, q = ((0, i), (5, i), (i, 0), (i, 5))[d]
                    value = hrecv[t, c, d, 1, SPOT[i], :, ds].astype(F32) + uext[s + 1, q + 1, :, ls]
                    if i == 0:
                        value = value + cu[(0, 2, 0, 1)[d]]
                    if i == SIDE - 1:
                        value = value + cu[(1, 3, 2, 3)[d]]
                    value = jnp.where(oks[d], value, 0.0).astype(BF16)
                    s, q = ((0, i + 1), (7, i + 1), (i + 1, 0), (i + 1, 7))[d]
                    loc[s, q, :, ls] = value
            for d in range(4):
                sd, qd = ((0, 2), (0, 3), (1, 2), (1, 3))[d]
                si, qi = ((0, 0), (5, 0), (0, 5), (5, 5))[d]
                value = corners[t, c, d, 1, :, ds].astype(F32)
                value = value + hrecv[t, c, sd, 0, SPOT[si], :, ds].astype(F32)
                value = value + hrecv[t, c, qd, 0, SPOT[qi], :, ds].astype(F32)
                value = jnp.where(diag_ok[d], value, 0.0).astype(BF16)
                s, q = ((0, 0), (0, 7), (7, 0), (7, 7))[d]
                loc[s, q, :, ls] = value

    own_offset = offs[m]
    own_count = jnp.where(m == MEMBERS - 1, KGROUP, offs[jnp.minimum(m + 1, MEMBERS - 1)]) - own_offset

    def tables():
        slot = iota((KGROUP, KMAX), 0)
        k = iota((KGROUP, KMAX), 1)
        for j in range(MEMBERS):
            first = offs[j]
            limit = (KGROUP if j == MEMBERS - 1 else offs[j + 1]) - first
            place[:, j * KMAX:(j + 1) * KMAX] = one_hot(
                jnp.logical_and(slot == first + k, k < limit)
            )
        k = iota((KMAX, KGROUP), 0)
        index = iota((KMAX, KGROUP), 1)
        slot = (index % SHARE) * MEMBERS + index // SHARE
        pick[...] = one_hot(jnp.logical_and(slot == own_offset + k, k < own_count))

    def expand_basis():
        j, i = iota((PADSLAB, SLAB), 0), iota((PADSLAB, SLAB), 1)
        spread = one_hot(
            jnp.logical_and(i == (j // CELL) * ROWS + j % CELL, j % CELL < ROWS)
        )
        for s in range(EXT):
            part = dot(spread, braw[s * SLAB:(s + 1) * SLAB, :])
            bt[:, s * PADSLAB:(s + 1) * PADSLAB] = part.T.astype(BF16)
            if 1 <= s <= SIDE:
                bint[(s - 1) * INNER:s * INNER, :] = part[CELL:CELL + INNER, :].astype(BF16)

    def expand_inverse():
        j, i = iota((INNER, INNER), 0), iota((INNER, INNER), 1)
        spread = one_hot(
            jnp.logical_and(i == 6 + (j // CELL) * ROWS + j % CELL, j % CELL < ROWS)
        )

        def step(s, carry):
            wp[pl.ds(pl.multiple_of(s * INNER, INNER), INNER), :] = dot(
                spread, wraw[s]
            ).astype(BF16)
            return carry

        lax.fori_loop(0, SIDE, step, 0)

    def gather_one(t, c):
        return [
            remote(
                pieces.at[t, c, m], pieces.at[t, c, m],
                g1_s.at[t, c, j], g1_r.at[t, c, j], group_to[j],
            )
            for j in GORDER
        ]

    def gather_two(t, c):
        return [
            remote(
                cvals.at[t, c, m], cvals.at[t, c, m],
                g2_s.at[t, c, j], g2_r.at[t, c, j], group_to[j],
            )
            for j in GORDER
        ]

    def restrict(t, c):
        ls = pl.ds(c * width, width)
        local = loc[:, :, :, ls].reshape(EXT * PADSLAB, width)
        projected = dot(bt[...], local)
        keep = iota((KMAX, width), 0) < own_count
        pieces[t, c, m] = jnp.where(keep, projected, 0.0).astype(BF16)

    def fine_product(c):
        ls = pl.ds(c * width, width)
        i, j = iota((SLAB, PADSLAB), 0), iota((SLAB, PADSLAB), 1)
        pack = one_hot(
            jnp.logical_and(i == (j // CELL) * ROWS + j % CELL, j % CELL < ROWS)
        )
        for s in range(EXT):
            locc[s * SLAB:(s + 1) * SLAB, ls] = dot(
                pack, loc[s, :, :, ls].reshape(PADSLAB, width)
            ).astype(BF16)
        fine[:, ls] = dot(wp[...], locc[:, ls])

    def core_copies(t, c):
        return [
            remote(
                cores.at[t, c, h], corer.at[t, c, h],
                core_s.at[t, c, h], core_r.at[t, c, h], core_to,
            )
            for h in range(2)
        ]

    def y_copies(t, c):
        return [
            remote(
                ysend.at[t, c, k], yrecv.at[t, c, k],
                y_s.at[t, c, k], y_r.at[t, c, k], y_to,
            )
            for k in range(NZ)
        ]

    def z_copies(t, c):
        return [
            remote(
                zsend.at[t, c, k], zrecv.at[t, c, k],
                z_s.at[t, c, k], z_r.at[t, c, k], z_to[k],
            )
            for k in range(NZ)
        ]

    def block(t, c, own, half):
        side = core if own else 1 - core
        return cbuf[side, pl.ds(half * NZ, NZ)].reshape(NZ * SHARE, KGROUP)

    def coarse(t, c):
        coef[:, pl.ds(c * width, width)] = dot(
            place[...], pieces[t, c].reshape(MEMBERS * KMAX, width)
        ).astype(BF16)
        copies = core_copies(t, c)

        def product(own, half):
            return dot(block(t, c, own, half), coef[:, pl.ds(c * width, width)]).reshape(
                NZ, SHARE, width
            )

        cores[t, c, 0] = product(False, 1 - ylo).astype(BF16)
        copies[0].start()
        pb[c, 0] = product(True, 1 - ylo)
        cores[t, c, 1] = product(False, ylo).astype(BF16)
        copies[1].start()

    def reduce_sums(t, c):
        copies, ys, zs = core_copies(t, c), y_copies(t, c), z_copies(t, c)
        with jax.named_scope("core0"):
            copies[0].wait_recv()
        with jax.named_scope("ysend"):
            for k in ZORDER:
                zz = lax.rem(z + k, NZ)
                ysend[t, c, k] = (pb[c, 0, zz] + corer[t, c, 0, zz].astype(F32)).astype(BF16)
                ys[k].start()
            pb[c, 1] = dot(block(t, c, True, ylo), coef[:, pl.ds(c * width, width)]).reshape(
                NZ, SHARE, width
            )
        with jax.named_scope("core1"):
            copies[1].wait_recv()
        with jax.named_scope("ywait"):
            for k in ZORDER:
                zz = lax.rem(z + k, NZ)
                ys[k].wait_recv()
                value = pb[c, 1, zz] + corer[t, c, 1, zz].astype(F32) + yrecv[t, c, k].astype(F32)
                if k == 0:
                    total = value
                else:
                    zsend[t, c, k] = value.astype(BF16)
                    zs[k].start()
        with jax.named_scope("zwait"):
            for k in ZORDER[::-1]:
                if k:
                    zs[k].wait_recv()
                    total = total + zrecv[t, c, k].astype(F32)
            cvals[t, c, m] = total.astype(BF16)

    def correct(t, c):
        ls = pl.ds(c * width, width)
        chosen = dot(pick[...], cvals[t, c].reshape(MEMBERS * SHARE, width)).astype(BF16)
        for s in range(SIDE):
            rows = slice(s * INNER, (s + 1) * INNER)
            total = fine[rows, ls] + dot(bint[rows, :], chosen)
            total = total.reshape(SIDE, CELL, width)
            if t == 0:
                sol[s, :, :, ls] = uext[s + 1, 1:1 + SIDE, :, ls] + total
                uext[s + 1, 1:1 + SIDE, :, ls] = total
            else:
                sol[s, :, :, ls] = sol[s, :, :, ls] + total
                for q in range(SIDE):
                    for lane, _ in lane_tiles(c):
                        for comp_id in range(3):
                            out[s, q, :, comp_id, pl.ds(lane, 128)] = sol[
                                s, q, pl.ds(comp_id * 10, 10), pl.ds(lane, 128)
                            ]

    def start_all(copies):
        for copy in copies:
            copy.start()

    def recv_all(copies):
        for copy in copies:
            copy.wait_recv()

    def scoped(name, func, *args):
        with jax.named_scope(name):
            func(*args)

    chunks = range(nch)
    scoped("load0", loads[0].wait)
    scoped("load0", loads[1].wait)
    scoped("unpack", unpack_inputs)
    for c in chunks:
        scoped("stencil", stencil, 0, c)
    scoped("barrier", pl.semaphore_wait, barrier, len(partners))
    for t in range(SWEEPS):
        for c in chunks:
            if t:
                scoped("stencil", stencil, t, c)
            for part in range(2):
                scoped("halo_send", start_all, halo_copies(t, c, part, (2, 3)))
                scoped("halo_send", start_all, halo_copies(t, c, part, (0, 1)))
        if t == 0:
            scoped("tables", tables)
            scoped("load1", loads[2].wait)
            scoped("basis", expand_basis)
        for c in chunks:
            scoped("end_wait", recv_all, halo_copies(t, c, 0, (2, 3)))
            scoped("end_send", start_all, corner_copies(t, c))
        if t == 0:
            for copy in loads[3:]:
                scoped("load2", copy.wait)
            scoped("inverse", expand_inverse)
        for c in chunks:
            scoped("halo_s", recv_all, halo_copies(t, c, 0, (0, 1)) + halo_copies(t, c, 1, (0, 1)))
            scoped("halo_q", recv_all, halo_copies(t, c, 1, (2, 3)))
            scoped("corner", recv_all, corner_copies(t, c))
            scoped("finish", finish_residual, t, c)
            scoped("restrict", restrict, t, c)
            scoped("g1_send", start_all, gather_one(t, c))
        for c in chunks:
            scoped("fine", fine_product, c)
        for c in chunks:
            scoped("g1_wait", recv_all, gather_one(t, c))
            scoped("coarse", coarse, t, c)
        for c in chunks:
            reduce_sums(t, c)
            scoped("g2_send", start_all, gather_two(t, c))
        for c in chunks:
            scoped("g2_wait", recv_all, gather_two(t, c))
            scoped("correct", correct, t, c)
    for t in range(SWEEPS):
        for c in chunks:
            for copy in (
                halo_copies(t, c, 0, range(4)) + halo_copies(t, c, 1, range(4))
                + corner_copies(t, c)
                + gather_one(t, c) + core_copies(t, c)
                + y_copies(t, c) + z_copies(t, c)[1:] + gather_two(t, c)
            ):
                copy.wait_send()


def shards(nch, rhs, start, stiffness, sub_inverse, basis, coarse_inverse, offsets):
    def held(array):
        return pltpu.with_memory_space_constraint(array, pltpu.HBM)

    def turned(field):
        return jnp.transpose(field, (0, 1, 3, 2, 4))

    width = LANES // nch
    lead = (SWEEPS, nch)
    vmem = pl.BlockSpec(memory_space=pltpu.VMEM)
    hbm = pl.BlockSpec(memory_space=pl.ANY)
    dma = pltpu.SemaphoreType.DMA
    out = pl.pallas_call(
        functools.partial(kernel, nch),
        name="schwarz",
        out_shape=jax.ShapeDtypeStruct((SIDE, SIDE, 10, 3, LANES), F32),
        in_specs=[pl.BlockSpec(memory_space=pltpu.SMEM), hbm, hbm, vmem, hbm, hbm, hbm],
        out_specs=vmem,
        scratch_shapes=[
            pltpu.VMEM((SIDE, SIDE, 10, 3, LANES), F32),
            pltpu.VMEM((SIDE, SIDE, 10, 3, LANES), F32),
            pltpu.VMEM((SIDE, SIDE, CELL, 128), F32),
            pltpu.VMEM((SIDE, SIDE, CELL, LANES), F32),
            pltpu.VMEM((EXT, EXT, CELL, LANES), F32),
            pltpu.VMEM((SIDE, SIDE, CELL, LANES), F32),
            pltpu.VMEM((EXT, EXT, CELL, LANES), BF16),
            pltpu.VMEM((NLOC, LANES), BF16),
            pltpu.VMEM((SIDE, INNER, NLOC), BF16),
            pltpu.VMEM((SIDE * INNER, NLOC), BF16),
            pltpu.VMEM((NLOC, KMAX), BF16),
            pltpu.VMEM((SIDE * INNER, KMAX), BF16),
            pltpu.VMEM((KMAX, EXT * PADSLAB), BF16),
            pltpu.VMEM((2, 2 * NZ, SHARE, KGROUP), BF16),
            pltpu.VMEM((KGROUP, LANES), BF16),
            pltpu.VMEM((KGROUP, MEMBERS * KMAX), BF16),
            pltpu.VMEM((KMAX, KGROUP), BF16),
            pltpu.VMEM((SIDE * INNER, LANES), F32),
            pltpu.VMEM((nch, 2, NZ, SHARE, width), F32),
            pltpu.VMEM(lead + (4, 2, SIDE, CELL, width), BF16),
            pltpu.VMEM(lead + (4, 2, SIDE, CELL, width), BF16),
            pltpu.VMEM(lead + (4, 2, CELL, width), BF16),
            pltpu.VMEM(lead + (MEMBERS, KMAX, width), BF16),
            pltpu.VMEM(lead + (2, NZ, SHARE, width), BF16),
            pltpu.VMEM(lead + (2, NZ, SHARE, width), BF16),
            pltpu.VMEM(lead + (NZ, SHARE, width), BF16),
            pltpu.VMEM(lead + (NZ, SHARE, width), BF16),
            pltpu.VMEM(lead + (NZ, SHARE, width), BF16),
            pltpu.VMEM(lead + (NZ, SHARE, width), BF16),
            pltpu.VMEM(lead + (MEMBERS, SHARE, width), BF16),
            dma((5 + SIDE,)),
            dma(lead + (2, 4)), dma(lead + (2, 4)),
            dma(lead + (4,)), dma(lead + (4,)),
            dma(lead + (8,)), dma(lead + (8,)),
            dma(lead + (2,)), dma(lead + (2,)),
            dma(lead + (8,)), dma(lead + (8,)),
            dma(lead + (8,)), dma(lead + (8,)),
            dma(lead + (8,)), dma(lead + (8,)),
        ],
        compiler_params=pltpu.CompilerParams(
            collective_id=0, has_side_effects=True, vmem_limit_bytes=44 * 1024 * 1024
        ),
    )(
        held(offsets[0]),
        held(turned(start)),
        held(turned(rhs)),
        held(stiffness),
        held(sub_inverse[0]),
        held(basis[0]),
        held(coarse_inverse.reshape(2 * NZ, 2, SHARE, KGROUP)),
    )
    return turned(out)


def solution(mesh):
    return jax.shard_map(
        functools.partial(shards, 1),
        mesh=mesh,
        in_specs=(
            P("sub", ("crow", "ccol"), None, None, None),
            P("sub", ("crow", "ccol"), None, None, None),
            P("sub", ("crow", "ccol"), None, None),
            P(("sub", "crow", "ccol"), None, None),
            P(("sub", "crow", "ccol"), None, None),
            P(None, ("crow", "ccol"), "sub"),
            P("sub", None),
        ),
        out_specs=P("sub", ("crow", "ccol"), None, None, None),
        check_vma=False,
    )
```

```python
import functools

import jax
import jax.numpy as jnp
from jax import lax
from jax.experimental import pallas as pl
from jax.experimental.pallas import tpu as pltpu
from jax.sharding import PartitionSpec as P

MESH = pl.DeviceIdType.MESH
SWEEPS = 2
SIDE = 6
EXT = 8
ROWS = 30
CELL = 32
SLAB = EXT * ROWS
PADSLAB = EXT * CELL
INNER = SIDE * CELL
NLOC = EXT * SLAB
LANES = 256
MEMBERS = 8
KMAX = 128
KGROUP = 512
SHARE = 64
NZ = 8
ZORDER = (4, 3, 5, 2, 6, 1, 7, 0)
SPOT = (0, 2, 3, 4, 5, 1)
GORDER = (5, 3, 7, 1, 4, 2, 6)
F32 = jnp.float32
BF16 = jnp.bfloat16


def iota(shape, dim):
    return lax.broadcasted_iota(jnp.int32, shape, dim)


def one_hot(mask):
    return jnp.where(mask, 1.0, 0.0).astype(BF16)


def dot(a, b):
    return jnp.dot(a, b, preferred_element_type=F32)


def kernel(
    nch,
    offs,
    start_hbm,
    rhs_hbm,
    stiff,
    w_hbm,
    basis_hbm,
    c_hbm,
    out,
    start_raw,
    rhs_raw,
    diag,
    sol,
    uext,
    res,
    loc,
    locc,
    wraw,
    wp,
    braw,
    bint,
    bt,
    cbuf,
    coef,
    place,
    pick,
    fine,
    pb,
    hsend,
    hrecv,
    corners,
    pieces,
    cores,
    corer,
    ysend,
    yrecv,
    zsend,
    zrecv,
    cvals,
    load_sem,
    halo_s,
    halo_r,
    corner_s,
    corner_r,
    g1_s,
    g1_r,
    core_s,
    core_r,
    y_s,
    y_r,
    z_s,
    z_r,
    g2_s,
    g2_r,
):
    width = LANES // nch
    g = lax.axis_index("sub")
    crow = lax.axis_index("crow")
    ccol = lax.axis_index("ccol")
    m = crow * 2 + ccol
    core = lax.rem(g, 2)
    z = lax.rem(g // 2, NZ)
    ylo = g // (2 * NZ)

    def at(gg, mm):
        return (gg, mm // 2, lax.rem(mm, 2))

    def sub_of(yy, zz, cc):
        return (yy * NZ + zz) * 2 + cc

    gp, gm = lax.rem(g + 1, 32), lax.rem(g + 31, 32)
    mp, mm = lax.rem(m + 1, MEMBERS), lax.rem(m + 7, MEMBERS)
    halo_to = [at(gp, m), at(gm, m), at(g, mp), at(g, mm)]
    group_to = [at(g, lax.rem(m + j, MEMBERS)) for j in range(MEMBERS)]
    core_to = at(sub_of(ylo, z, 1 - core), m)
    y_to = at(sub_of(1 - ylo, z, core), m)
    z_to = [at(sub_of(ylo, lax.rem(z + k, NZ), core), m) for k in range(NZ)]
    partners = halo_to + group_to[1:] + [core_to, y_to] + z_to[1:]

    barrier = pltpu.get_barrier_semaphore()
    for device in partners:
        pl.semaphore_signal(barrier, inc=1, device_id=device, device_id_type=MESH)

    loads = [
        pltpu.make_async_copy(start_hbm, start_raw, load_sem.at[0]),
        pltpu.make_async_copy(rhs_hbm, rhs_raw, load_sem.at[4 + SIDE]),
        pltpu.make_async_copy(basis_hbm, braw, load_sem.at[1]),
        pltpu.make_async_copy(c_hbm.at[:, 0], cbuf.at[0], load_sem.at[2]),
        pltpu.make_async_copy(c_hbm.at[:, 1], cbuf.at[1], load_sem.at[3]),
    ] + [
        pltpu.make_async_copy(
            w_hbm.at[pl.ds((s + 1) * SLAB + 24, INNER)], wraw.at[s], load_sem.at[4 + s]
        )
        for s in range(SIDE)
    ]
    for copy in loads:
        copy.start()

    zero_row = jnp.zeros((EXT, CELL, LANES), F32)
    uext[0] = zero_row
    uext[EXT - 1] = zero_row
    for s in range(1, EXT - 1):
        uext[s, 0] = zero_row[0]
        uext[s, EXT - 1] = zero_row[0]
        uext[s, 1:EXT - 1, 24:CELL, :] = jnp.zeros((SIDE, CELL - 24, LANES), F32)

    row = iota((CELL, 128), 0)
    layer = lax.rem(row, 10)
    has_below = layer != 0
    has_above = jnp.logical_and(layer != 9, row < ROWS)
    ok_sm, ok_sp, ok_qm, ok_qp = g > 0, g < 31, m > 0, m < MEMBERS - 1

    def remote(src, dst, send, recv, device):
        return pltpu.make_async_remote_copy(
            src_ref=src,
            dst_ref=dst,
            send_sem=send,
            recv_sem=recv,
            device_id=device,
            device_id_type=MESH,
        )

    def halo_copies(t, c, part, sides):
        where = pl.ds(0, 2) if part == 0 else pl.ds(2, 4)
        return [
            remote(
                hsend.at[t, c, d, :, where], hrecv.at[t, c, d, :, where],
                halo_s.at[t, c, part, d], halo_r.at[t, c, part, d], halo_to[d],
            )
            for d in sides
        ]

    def corner_copies(t, c):
        return [
            remote(
                hrecv.at[t, c, side, :, end], corners.at[t, c, d],
                corner_s.at[t, c, d], corner_r.at[t, c, d], halo_to[to],
            )
            for d, side, end, to in ((0, 2, 1, 0), (1, 3, 1, 0), (2, 2, 0, 1), (3, 3, 0, 1))
        ]

    def unpack_inputs():
        first = lax.rem(iota((CELL, 10), 0), 10) == iota((CELL, 10), 1)
        comp = iota((CELL, 10), 0) // 10

        def step(s, carry):
            for q in range(SIDE):
                k = stiff[s, q]
                spread = jnp.where(comp == 0, k[0:1], jnp.where(comp == 1, k[1:2], k[2:3]))
                column = jnp.sum(jnp.where(first, spread, 0.0), axis=1, keepdims=True)
                diag[s, q] = jnp.broadcast_to(6.0 + column, (CELL, 128))
                for lane in range(0, LANES, 128):
                    ls = pl.ds(lane, 128)
                    res[s, q, pl.ds(24, 8), ls] = jnp.zeros((8, 128), F32)
                    for comp_id in range(3):
                        rows = pl.ds(comp_id * 10, 10)
                        uext[s + 1, q + 1, rows, ls] = start_raw[s, q, :, comp_id, ls]
                        res[s, q, rows, ls] = rhs_raw[s, q, :, comp_id, ls]
            return carry

        lax.fori_loop(0, SIDE, step, 0)

    def lane_tiles(c):
        return [(c * width + i * 128, i * 128) for i in range(width // 128)]

    def stencil(t, c):
        def step(s, carry):
            for lane, _ in lane_tiles(c):
                ls = pl.ds(lane, 128)
                for q in range(SIDE):
                    u = uext[s + 1, q + 1, :, ls]
                    beside = (
                        uext[s, q + 1, :, ls] + uext[s + 2, q + 1, :, ls]
                        + uext[s + 1, q, :, ls] + uext[s + 1, q + 2, :, ls]
                    )
                    beside = beside + jnp.where(has_below, pltpu.roll(u, 1, 0), 0.0)
                    beside = beside + jnp.where(has_above, pltpu.roll(u, CELL - 1, 0), 0.0)
                    res[s, q, :, ls] = res[s, q, :, ls] - (diag[s, q] * u - beside)
            return carry

        lax.fori_loop(0, SIDE, step, 0)
        for lane, dst in lane_tiles(c):
            ls, ds = pl.ds(lane, 128), pl.ds(dst, 128)
            for i in range(SIDE):
                for d, (s, q) in enumerate(((SIDE - 1, i), (0, i), (i, SIDE - 1), (i, 0))):
                    hsend[t, c, d, 0, SPOT[i], :, ds] = uext[s + 1, q + 1, :, ls].astype(BF16)
                    hsend[t, c, d, 1, SPOT[i], :, ds] = res[s, q, :, ls].astype(BF16)

    def finish_residual(t, c):
        for lane, dst in lane_tiles(c):
            ls, ds = pl.ds(lane, 128), pl.ds(dst, 128)

            def got(d, field, i, ok):
                return jnp.where(ok, hrecv[t, c, d, field, SPOT[i], :, ds].astype(F32), 0.0)

            def corner(d, field, ok):
                return jnp.where(ok, corners[t, c, d, field, :, ds].astype(F32), 0.0)

            oks = (ok_sm, ok_sp, ok_qm, ok_qp)
            diag_ok = (
                jnp.logical_and(ok_sm, ok_qm), jnp.logical_and(ok_sm, ok_qp),
                jnp.logical_and(ok_sp, ok_qm), jnp.logical_and(ok_sp, ok_qp),
            )
            cu = [corner(d, 0, diag_ok[d]) for d in range(4)]
            for s in range(SIDE):
                for q in range(SIDE):
                    value = res[s, q, :, ls]
                    edge = False
                    for d, here, i in ((0, s == 0, q), (1, s == 5, q), (2, q == 0, s), (3, q == 5, s)):
                        if here:
                            value = value + got(d, 0, i, oks[d])
                            edge = True
                    if edge:
                        res[s, q, :, ls] = value
                    loc[s + 1, q + 1, :, ls] = value.astype(BF16)
            for d in range(4):
                for i in range(SIDE):
                    s, q = ((0, i), (5, i), (i, 0), (i, 5))[d]
                    value = hrecv[t, c, d, 1, SPOT[i], :, ds].astype(F32) + uext[s + 1, q + 1, :, ls]
                    if i == 0:
                        value = value + cu[(0, 2, 0, 1)[d]]
                    if i == SIDE - 1:
                        value = value + cu[(1, 3, 2, 3)[d]]
                    value = jnp.where(oks[d], value, 0.0).astype(BF16)
                    s, q = ((0, i + 1), (7, i + 1), (i + 1, 0), (i + 1, 7))[d]
                    loc[s, q, :, ls] = value
            for d in range(4):
                sd, qd = ((0, 2), (0, 3), (1, 2), (1, 3))[d]
                si, qi = ((0, 0), (5, 0), (0, 5), (5, 5))[d]
                value = corners[t, c, d, 1, :, ds].astype(F32)
                value = value + hrecv[t, c, sd, 0, SPOT[si], :, ds].astype(F32)
                value = value + hrecv[t, c, qd, 0, SPOT[qi], :, ds].astype(F32)
                value = jnp.where(diag_ok[d], value, 0.0).astype(BF16)
                s, q = ((0, 0), (0, 7), (7, 0), (7, 7))[d]
                loc[s, q, :, ls] = value

    own_offset = offs[m]
    own_count = jnp.where(m == MEMBERS - 1, KGROUP, offs[jnp.minimum(m + 1, MEMBERS - 1)]) - own_offset

    def tables():
        slot = iota((KGROUP, KMAX), 0)
        k = iota((KGROUP, KMAX), 1)
        for j in range(MEMBERS):
            first = offs[j]
            limit = (KGROUP if j == MEMBERS - 1 else offs[j + 1]) - first
            place[:, j * KMAX:(j + 1) * KMAX] = one_hot(
                jnp.logical_and(slot == first + k, k < limit)
            )
        k = iota((KMAX, KGROUP), 0)
        index = iota((KMAX, KGROUP), 1)
        slot = (index % SHARE) * MEMBERS + index // SHARE
        pick[...] = one_hot(jnp.logical_and(slot == own_offset + k, k < own_count))

    def expand_basis():
        j, i = iota((PADSLAB, SLAB), 0), iota((PADSLAB, SLAB), 1)
        spread = one_hot(
            jnp.logical_and(i == (j // CELL) * ROWS + j % CELL, j % CELL < ROWS)
        )
        for s in range(EXT):
            part = dot(spread, braw[s * SLAB:(s + 1) * SLAB, :])
            bt[:, s * PADSLAB:(s + 1) * PADSLAB] = part.T.astype(BF16)
            if 1 <= s <= SIDE:
                bint[(s - 1) * INNER:s * INNER, :] = part[CELL:CELL + INNER, :].astype(BF16)

    def expand_inverse():
        j, i = iota((INNER, INNER), 0), iota((INNER, INNER), 1)
        spread = one_hot(
            jnp.logical_and(i == 6 + (j // CELL) * ROWS + j % CELL, j % CELL < ROWS)
        )

        def step(s, carry):
            wp[pl.ds(pl.multiple_of(s * INNER, INNER), INNER), :] = dot(
                spread, wraw[s]
            ).astype(BF16)
            return carry

        lax.fori_loop(0, SIDE, step, 0)

    def gather_one(t, c):
        return [
            remote(
                pieces.at[t, c, m], pieces.at[t, c, m],
                g1_s.at[t, c, j], g1_r.at[t, c, j], group_to[j],
            )
            for j in GORDER
        ]

    def gather_two(t, c):
        return [
            remote(
                cvals.at[t, c, m], cvals.at[t, c, m],
                g2_s.at[t, c, j], g2_r.at[t, c, j], group_to[j],
            )
            for j in GORDER
        ]

    def restrict(t, c):
        ls = pl.ds(c * width, width)
        local = loc[:, :, :, ls].reshape(EXT * PADSLAB, width)
        projected = dot(bt[...], local)
        keep = iota((KMAX, width), 0) < own_count
        pieces[t, c, m] = jnp.where(keep, projected, 0.0).astype(BF16)

    def fine_product(c):
        ls = pl.ds(c * width, width)
        i, j = iota((SLAB, PADSLAB), 0), iota((SLAB, PADSLAB), 1)
        pack = one_hot(
            jnp.logical_and(i == (j // CELL) * ROWS + j % CELL, j % CELL < ROWS)
        )
        for s in range(EXT):
            locc[s * SLAB:(s + 1) * SLAB, ls] = dot(
                pack, loc[s, :, :, ls].reshape(PADSLAB, width)
            ).astype(BF16)
        fine[:, ls] = dot(wp[...], locc[:, ls])

    def core_copies(t, c):
        return [
            remote(
                cores.at[t, c, h], corer.at[t, c, h],
                core_s.at[t, c, h], core_r.at[t, c, h], core_to,
            )
            for h in range(2)
        ]

    def y_copies(t, c):
        return [
            remote(
                ysend.at[t, c, k], yrecv.at[t, c, k],
                y_s.at[t, c, k], y_r.at[t, c, k], y_to,
            )
            for k in range(NZ)
        ]

    def z_copies(t, c):
        return [
            remote(
                zsend.at[t, c, k], zrecv.at[t, c, k],
                z_s.at[t, c, k], z_r.at[t, c, k], z_to[k],
            )
            for k in range(NZ)
        ]

    def block(t, c, own, half):
        side = core if own else 1 - core
        return cbuf[side, pl.ds(half * NZ, NZ)].reshape(NZ * SHARE, KGROUP)

    def coarse(t, c):
        coef[:, pl.ds(c * width, width)] = dot(
            place[...], pieces[t, c].reshape(MEMBERS * KMAX, width)
        ).astype(BF16)
        copies = core_copies(t, c)

        def product(own, half):
            return dot(block(t, c, own, half), coef[:, pl.ds(c * width, width)]).reshape(
                NZ, SHARE, width
            )

        cores[t, c, 0] = product(False, 1 - ylo).astype(BF16)
        copies[0].start()
        pb[c, 0] = product(True, 1 - ylo)
        cores[t, c, 1] = product(False, ylo).astype(BF16)
        copies[1].start()

    def reduce_core(t, c):
        copies, ys = core_copies(t, c), y_copies(t, c)
        copies[0].wait_recv()
        for k in ZORDER:
            zz = lax.rem(z + k, NZ)
            ysend[t, c, k] = (pb[c, 0, zz] + corer[t, c, 0, zz].astype(F32)).astype(BF16)
            ys[k].start()
        pb[c, 1] = dot(block(t, c, True, ylo), coef[:, pl.ds(c * width, width)]).reshape(
            NZ, SHARE, width
        )

    def reduce_y(t, c):
        copies, ys, zs = core_copies(t, c), y_copies(t, c), z_copies(t, c)
        copies[1].wait_recv()
        for k in ZORDER:
            zz = lax.rem(z + k, NZ)
            ys[k].wait_recv()
            value = pb[c, 1, zz] + corer[t, c, 1, zz].astype(F32) + yrecv[t, c, k].astype(F32)
            if k == 0:
                pb[c, 0, 0] = value
            else:
                zsend[t, c, k] = value.astype(BF16)
                zs[k].start()

    def reduce_z(t, c):
        zs = z_copies(t, c)
        total = pb[c, 0, 0]
        for k in ZORDER[::-1]:
            if k:
                zs[k].wait_recv()
                total = total + zrecv[t, c, k].astype(F32)
        cvals[t, c, m] = total.astype(BF16)

    def correct(t, c):
        ls = pl.ds(c * width, width)
        chosen = dot(pick[...], cvals[t, c].reshape(MEMBERS * SHARE, width)).astype(BF16)
        for s in range(SIDE):
            rows = slice(s * INNER, (s + 1) * INNER)
            total = fine[rows, ls] + dot(bint[rows, :], chosen)
            total = total.reshape(SIDE, CELL, width)
            if t == 0:
                sol[s, :, :, ls] = uext[s + 1, 1:1 + SIDE, :, ls] + total
                uext[s + 1, 1:1 + SIDE, :, ls] = total
            else:
                sol[s, :, :, ls] = sol[s, :, :, ls] + total
                for q in range(SIDE):
                    for lane, _ in lane_tiles(c):
                        for comp_id in range(3):
                            out[s, q, :, comp_id, pl.ds(lane, 128)] = sol[
                                s, q, pl.ds(comp_id * 10, 10), pl.ds(lane, 128)
                            ]

    def start_all(copies):
        for copy in copies:
            copy.start()

    def recv_all(copies):
        for copy in copies:
            copy.wait_recv()

    def scoped(name, func, *args):
        with jax.named_scope(name):
            func(*args)

    chunks = range(nch)
    scoped("load0", loads[0].wait)
    scoped("load0", loads[1].wait)
    scoped("unpack", unpack_inputs)
    for c in chunks:
        scoped("stencil", stencil, 0, c)
    scoped("barrier", pl.semaphore_wait, barrier, len(partners))
    for c in chunks:
        for part in range(2):
            scoped("halo_send", start_all, halo_copies(0, c, part, (2, 3, 0, 1)))
    for t in range(SWEEPS):
        if t == 0:
            scoped("tables", tables)
            scoped("load1", loads[2].wait)
            scoped("basis", expand_basis)
        def residual_part(c):
            scoped("end_wait", recv_all, halo_copies(t, c, 0, (2, 3)))
            scoped("end_send", start_all, corner_copies(t, c))

        def restrict_part(c):
            for part in range(2):
                scoped("halo_s", recv_all, halo_copies(t, c, part, (0, 1)))
            scoped("halo_q", recv_all, halo_copies(t, c, 1, (2, 3)))
            scoped("corner", recv_all, corner_copies(t, c))
            scoped("finish", finish_residual, t, c)
            scoped("restrict", restrict, t, c)
            scoped("g1_send", start_all, gather_one(t, c))

        def coarse_part(c):
            scoped("g1_wait", recv_all, gather_one(t, c))
            scoped("coarse", coarse, t, c)

        residual_part(0)
        if t == 0:
            for copy in loads[3:]:
                scoped("load2", copy.wait)
            scoped("inverse", expand_inverse)
        restrict_part(0)
        residual_part(1)
        restrict_part(1)
        scoped("fine", fine_product, 0)
        coarse_part(0)
        scoped("core", reduce_core, t, 0)
        coarse_part(1)
        scoped("core", reduce_core, t, 1)
        scoped("y0", reduce_y, t, 0)
        scoped("fine", fine_product, 1)
        scoped("y1", reduce_y, t, 1)
        for c in chunks:
            scoped("zwait", reduce_z, t, c)
            scoped("g2_send", start_all, gather_two(t, c))
        for c in chunks:
            scoped("g2_wait", recv_all, gather_two(t, c))
            scoped("correct", correct, t, c)
            if t == 0:
                scoped("stencil", stencil, 1, c)
                for part in range(2):
                    scoped("halo_send", start_all, halo_copies(1, c, part, (2, 3, 0, 1)))
    for t in range(SWEEPS):
        for c in chunks:
            for copy in (
                halo_copies(t, c, 0, range(4)) + halo_copies(t, c, 1, range(4))
                + corner_copies(t, c)
                + gather_one(t, c) + core_copies(t, c)
                + y_copies(t, c) + z_copies(t, c)[1:] + gather_two(t, c)
            ):
                copy.wait_send()


def shards(nch, rhs, start, stiffness, sub_inverse, basis, coarse_inverse, offsets):
    def held(array):
        return pltpu.with_memory_space_constraint(array, pltpu.HBM)

    def turned(field):
        return jnp.transpose(field, (0, 1, 3, 2, 4))

    width = LANES // nch
    lead = (SWEEPS, nch)
    vmem = pl.BlockSpec(memory_space=pltpu.VMEM)
    hbm = pl.BlockSpec(memory_space=pl.ANY)
    dma = pltpu.SemaphoreType.DMA
    out = pl.pallas_call(
        functools.partial(kernel, nch),
        name="schwarz",
        out_shape=jax.ShapeDtypeStruct((SIDE, SIDE, 10, 3, LANES), F32),
        in_specs=[pl.BlockSpec(memory_space=pltpu.SMEM), hbm, hbm, vmem, hbm, hbm, hbm],
        out_specs=vmem,
        scratch_shapes=[
            pltpu.VMEM((SIDE, SIDE, 10, 3, LANES), F32),
            pltpu.VMEM((SIDE, SIDE, 10, 3, LANES), F32),
            pltpu.VMEM((SIDE, SIDE, CELL, 128), F32),
            pltpu.VMEM((SIDE, SIDE, CELL, LANES), F32),
            pltpu.VMEM((EXT, EXT, CELL, LANES), F32),
            pltpu.VMEM((SIDE, SIDE, CELL, LANES), F32),
            pltpu.VMEM((EXT, EXT, CELL, LANES), BF16),
            pltpu.VMEM((NLOC, LANES), BF16),
            pltpu.VMEM((SIDE, INNER, NLOC), BF16),
            pltpu.VMEM((SIDE * INNER, NLOC), BF16),
            pltpu.VMEM((NLOC, KMAX), BF16),
            pltpu.VMEM((SIDE * INNER, KMAX), BF16),
            pltpu.VMEM((KMAX, EXT * PADSLAB), BF16),
            pltpu.VMEM((2, 2 * NZ, SHARE, KGROUP), BF16),
            pltpu.VMEM((KGROUP, LANES), BF16),
            pltpu.VMEM((KGROUP, MEMBERS * KMAX), BF16),
            pltpu.VMEM((KMAX, KGROUP), BF16),
            pltpu.VMEM((SIDE * INNER, LANES), F32),
            pltpu.VMEM((nch, 2, NZ, SHARE, width), F32),
            pltpu.VMEM(lead + (4, 2, SIDE, CELL, width), BF16),
            pltpu.VMEM(lead + (4, 2, SIDE, CELL, width), BF16),
            pltpu.VMEM(lead + (4, 2, CELL, width), BF16),
            pltpu.VMEM(lead + (MEMBERS, KMAX, width), BF16),
            pltpu.VMEM(lead + (2, NZ, SHARE, width), BF16),
            pltpu.VMEM(lead + (2, NZ, SHARE, width), BF16),
            pltpu.VMEM(lead + (NZ, SHARE, width), BF16),
            pltpu.VMEM(lead + (NZ, SHARE, width), BF16),
            pltpu.VMEM(lead + (NZ, SHARE, width), BF16),
            pltpu.VMEM(lead + (NZ, SHARE, width), BF16),
            pltpu.VMEM(lead + (MEMBERS, SHARE, width), BF16),
            dma((5 + SIDE,)),
            dma(lead + (2, 4)), dma(lead + (2, 4)),
            dma(lead + (4,)), dma(lead + (4,)),
            dma(lead + (8,)), dma(lead + (8,)),
            dma(lead + (2,)), dma(lead + (2,)),
            dma(lead + (8,)), dma(lead + (8,)),
            dma(lead + (8,)), dma(lead + (8,)),
            dma(lead + (8,)), dma(lead + (8,)),
        ],
        compiler_params=pltpu.CompilerParams(
            collective_id=0, has_side_effects=True, vmem_limit_bytes=44 * 1024 * 1024
        ),
    )(
        held(offsets[0]),
        held(turned(start)),
        held(turned(rhs)),
        held(stiffness),
        held(sub_inverse[0]),
        held(basis[0]),
        held(coarse_inverse.reshape(2 * NZ, 2, SHARE, KGROUP)),
    )
    return turned(out)


def solution(mesh):
    return jax.shard_map(
        functools.partial(shards, 2),
        mesh=mesh,
        in_specs=(
            P("sub", ("crow", "ccol"), None, None, None),
            P("sub", ("crow", "ccol"), None, None, None),
            P("sub", ("crow", "ccol"), None, None),
            P(("sub", "crow", "ccol"), None, None),
            P(("sub", "crow", "ccol"), None, None),
            P(None, ("crow", "ccol"), "sub"),
            P("sub", None),
        ),
        out_specs=P("sub", ("crow", "ccol"), None, None, None),
        check_vma=False,
    )
```

```python
import functools

import jax
import jax.numpy as jnp
from jax import lax
from jax.experimental import pallas as pl
from jax.experimental.pallas import tpu as pltpu
from jax.sharding import PartitionSpec as P

MESH = pl.DeviceIdType.MESH
SWEEPS = 2
SIDE = 6
EXT = 8
ROWS = 30
CELL = 32
SLAB = EXT * ROWS
PADSLAB = EXT * CELL
INNER = SIDE * CELL
NLOC = EXT * SLAB
LANES = 256
MEMBERS = 8
KMAX = 128
KGROUP = 512
SHARE = 64
NZ = 8
ZORDER = (4, 3, 5, 2, 6, 1, 7, 0)
SPOT = (0, 2, 3, 4, 5, 1)
GORDER = (5, 3, 7, 1, 4, 2, 6)
F32 = jnp.float32
BF16 = jnp.bfloat16


def iota(shape, dim):
    return lax.broadcasted_iota(jnp.int32, shape, dim)


def one_hot(mask):
    return jnp.where(mask, 1.0, 0.0).astype(BF16)


def dot(a, b):
    return jnp.dot(a, b, preferred_element_type=F32)


def kernel(
    nch,
    offs,
    start_hbm,
    rhs_hbm,
    stiff,
    w_hbm,
    basis_hbm,
    c_hbm,
    out,
    start_raw,
    rhs_raw,
    diag,
    sol,
    uext,
    res,
    loc,
    locc,
    wraw,
    wp,
    braw,
    bint,
    bt,
    cbuf,
    coef,
    place,
    pick,
    fine,
    pb,
    hsend,
    hrecv,
    corners,
    pieces,
    cores,
    corer,
    ysend,
    yrecv,
    zsend,
    zrecv,
    cvals,
    load_sem,
    halo_s,
    halo_r,
    corner_s,
    corner_r,
    g1_s,
    g1_r,
    core_s,
    core_r,
    y_s,
    y_r,
    z_s,
    z_r,
    g2_s,
    g2_r,
):
    width = LANES // nch
    g = lax.axis_index("sub")
    crow = lax.axis_index("crow")
    ccol = lax.axis_index("ccol")
    m = crow * 2 + ccol
    core = lax.rem(g, 2)
    z = lax.rem(g // 2, NZ)
    ylo = g // (2 * NZ)

    def at(gg, mm):
        return (gg, mm // 2, lax.rem(mm, 2))

    def sub_of(yy, zz, cc):
        return (yy * NZ + zz) * 2 + cc

    gp, gm = lax.rem(g + 1, 32), lax.rem(g + 31, 32)
    mp, mm = lax.rem(m + 1, MEMBERS), lax.rem(m + 7, MEMBERS)
    halo_to = [at(gp, m), at(gm, m), at(g, mp), at(g, mm)]
    group_to = [at(g, lax.rem(m + j, MEMBERS)) for j in range(MEMBERS)]
    core_to = at(sub_of(ylo, z, 1 - core), m)
    y_to = at(sub_of(1 - ylo, z, core), m)
    z_to = [at(sub_of(ylo, lax.rem(z + k, NZ), core), m) for k in range(NZ)]
    partners = halo_to + group_to[1:] + [core_to, y_to] + z_to[1:]

    barrier = pltpu.get_barrier_semaphore()
    for device in partners:
        pl.semaphore_signal(barrier, inc=1, device_id=device, device_id_type=MESH)

    loads = [
        pltpu.make_async_copy(start_hbm, start_raw, load_sem.at[0]),
        pltpu.make_async_copy(rhs_hbm, rhs_raw, load_sem.at[4 + SIDE]),
        pltpu.make_async_copy(basis_hbm, braw, load_sem.at[1]),
        pltpu.make_async_copy(c_hbm.at[:, 0], cbuf.at[0], load_sem.at[2]),
        pltpu.make_async_copy(c_hbm.at[:, 1], cbuf.at[1], load_sem.at[3]),
    ] + [
        pltpu.make_async_copy(
            w_hbm.at[pl.ds((s + 1) * SLAB + 24, INNER)], wraw.at[s], load_sem.at[4 + s]
        )
        for s in range(SIDE)
    ]
    for copy in loads:
        copy.start()

    zero_row = jnp.zeros((EXT, CELL, LANES), F32)
    uext[0] = zero_row
    uext[EXT - 1] = zero_row
    for s in range(1, EXT - 1):
        uext[s, 0] = zero_row[0]
        uext[s, EXT - 1] = zero_row[0]
        uext[s, 1:EXT - 1, 24:CELL, :] = jnp.zeros((SIDE, CELL - 24, LANES), F32)

    row = iota((CELL, 128), 0)
    layer = lax.rem(row, 10)
    has_below = layer != 0
    has_above = jnp.logical_and(layer != 9, row < ROWS)
    ok_sm, ok_sp, ok_qm, ok_qp = g > 0, g < 31, m > 0, m < MEMBERS - 1

    def remote(src, dst, send, recv, device):
        return pltpu.make_async_remote_copy(
            src_ref=src,
            dst_ref=dst,
            send_sem=send,
            recv_sem=recv,
            device_id=device,
            device_id_type=MESH,
        )

    def halo_copies(t, c, part, sides):
        where = pl.ds(0, 2) if part == 0 else pl.ds(2, 4)
        return [
            remote(
                hsend.at[t, c, d, :, where], hrecv.at[t, c, d, :, where],
                halo_s.at[t, c, part, d], halo_r.at[t, c, part, d], halo_to[d],
            )
            for d in sides
        ]

    def corner_copies(t, c):
        return [
            remote(
                hrecv.at[t, c, side, :, end], corners.at[t, c, d],
                corner_s.at[t, c, d], corner_r.at[t, c, d], halo_to[to],
            )
            for d, side, end, to in ((0, 2, 1, 0), (1, 3, 1, 0), (2, 2, 0, 1), (3, 3, 0, 1))
        ]

    def unpack_inputs():
        first = lax.rem(iota((CELL, 10), 0), 10) == iota((CELL, 10), 1)
        comp = iota((CELL, 10), 0) // 10

        def step(s, carry):
            for q in range(SIDE):
                k = stiff[s, q]
                spread = jnp.where(comp == 0, k[0:1], jnp.where(comp == 1, k[1:2], k[2:3]))
                column = jnp.sum(jnp.where(first, spread, 0.0), axis=1, keepdims=True)
                diag[s, q] = jnp.broadcast_to(6.0 + column, (CELL, 128))
                for lane in range(0, LANES, 128):
                    ls = pl.ds(lane, 128)
                    res[s, q, pl.ds(24, 8), ls] = jnp.zeros((8, 128), F32)
                    for comp_id in range(3):
                        rows = pl.ds(comp_id * 10, 10)
                        uext[s + 1, q + 1, rows, ls] = start_raw[s, q, :, comp_id, ls]
                        res[s, q, rows, ls] = rhs_raw[s, q, :, comp_id, ls]
            return carry

        lax.fori_loop(0, SIDE, step, 0)

    def lane_tiles(c):
        return [(c * width + i * 128, i * 128) for i in range(width // 128)]

    def stencil(t, c):
        def step(s, carry):
            for lane, _ in lane_tiles(c):
                ls = pl.ds(lane, 128)
                for q in range(SIDE):
                    u = uext[s + 1, q + 1, :, ls]
                    beside = (
                        uext[s, q + 1, :, ls] + uext[s + 2, q + 1, :, ls]
                        + uext[s + 1, q, :, ls] + uext[s + 1, q + 2, :, ls]
                    )
                    beside = beside + jnp.where(has_below, pltpu.roll(u, 1, 0), 0.0)
                    beside = beside + jnp.where(has_above, pltpu.roll(u, CELL - 1, 0), 0.0)
                    res[s, q, :, ls] = res[s, q, :, ls] - (diag[s, q] * u - beside)
            return carry

        lax.fori_loop(0, SIDE, step, 0)
        for lane, dst in lane_tiles(c):
            ls, ds = pl.ds(lane, 128), pl.ds(dst, 128)
            for i in range(SIDE):
                for d, (s, q) in enumerate(((SIDE - 1, i), (0, i), (i, SIDE - 1), (i, 0))):
                    hsend[t, c, d, 0, SPOT[i], :, ds] = uext[s + 1, q + 1, :, ls].astype(BF16)
                    hsend[t, c, d, 1, SPOT[i], :, ds] = res[s, q, :, ls].astype(BF16)

    def finish_residual(t, c):
        for lane, dst in lane_tiles(c):
            ls, ds = pl.ds(lane, 128), pl.ds(dst, 128)

            def got(d, field, i, ok):
                return jnp.where(ok, hrecv[t, c, d, field, SPOT[i], :, ds].astype(F32), 0.0)

            def corner(d, field, ok):
                return jnp.where(ok, corners[t, c, d, field, :, ds].astype(F32), 0.0)

            oks = (ok_sm, ok_sp, ok_qm, ok_qp)
            diag_ok = (
                jnp.logical_and(ok_sm, ok_qm), jnp.logical_and(ok_sm, ok_qp),
                jnp.logical_and(ok_sp, ok_qm), jnp.logical_and(ok_sp, ok_qp),
            )
            cu = [corner(d, 0, diag_ok[d]) for d in range(4)]
            for s in range(SIDE):
                for q in range(SIDE):
                    value = res[s, q, :, ls]
                    edge = False
                    for d, here, i in ((0, s == 0, q), (1, s == 5, q), (2, q == 0, s), (3, q == 5, s)):
                        if here:
                            value = value + got(d, 0, i, oks[d])
                            edge = True
                    if edge:
                        res[s, q, :, ls] = value
                    loc[s + 1, q + 1, :, ls] = value.astype(BF16)
            for d in range(4):
                for i in range(SIDE):
                    s, q = ((0, i), (5, i), (i, 0), (i, 5))[d]
                    value = hrecv[t, c, d, 1, SPOT[i], :, ds].astype(F32) + uext[s + 1, q + 1, :, ls]
                    if i == 0:
                        value = value + cu[(0, 2, 0, 1)[d]]
                    if i == SIDE - 1:
                        value = value + cu[(1, 3, 2, 3)[d]]
                    value = jnp.where(oks[d], value, 0.0).astype(BF16)
                    s, q = ((0, i + 1), (7, i + 1), (i + 1, 0), (i + 1, 7))[d]
                    loc[s, q, :, ls] = value
            for d in range(4):
                sd, qd = ((0, 2), (0, 3), (1, 2), (1, 3))[d]
                si, qi = ((0, 0), (5, 0), (0, 5), (5, 5))[d]
                value = corners[t, c, d, 1, :, ds].astype(F32)
                value = value + hrecv[t, c, sd, 0, SPOT[si], :, ds].astype(F32)
                value = value + hrecv[t, c, qd, 0, SPOT[qi], :, ds].astype(F32)
                value = jnp.where(diag_ok[d], value, 0.0).astype(BF16)
                s, q = ((0, 0), (0, 7), (7, 0), (7, 7))[d]
                loc[s, q, :, ls] = value

    own_offset = offs[m]
    own_count = jnp.where(m == MEMBERS - 1, KGROUP, offs[jnp.minimum(m + 1, MEMBERS - 1)]) - own_offset

    def tables():
        slot = iota((KGROUP, KMAX), 0)
        k = iota((KGROUP, KMAX), 1)
        for j in range(MEMBERS):
            first = offs[j]
            limit = (KGROUP if j == MEMBERS - 1 else offs[j + 1]) - first
            place[:, j * KMAX:(j + 1) * KMAX] = one_hot(
                jnp.logical_and(slot == first + k, k < limit)
            )
        k = iota((KMAX, KGROUP), 0)
        index = iota((KMAX, KGROUP), 1)
        slot = (index % SHARE) * MEMBERS + index // SHARE
        pick[...] = one_hot(jnp.logical_and(slot == own_offset + k, k < own_count))

    def expand_basis():
        j, i = iota((PADSLAB, SLAB), 0), iota((PADSLAB, SLAB), 1)
        spread = one_hot(
            jnp.logical_and(i == (j // CELL) * ROWS + j % CELL, j % CELL < ROWS)
        )
        for s in range(EXT):
            part = dot(spread, braw[s * SLAB:(s + 1) * SLAB, :])
            bt[:, s * PADSLAB:(s + 1) * PADSLAB] = part.T.astype(BF16)
            if 1 <= s <= SIDE:
                bint[(s - 1) * INNER:s * INNER, :] = part[CELL:CELL + INNER, :].astype(BF16)

    def expand_inverse():
        j, i = iota((INNER, INNER), 0), iota((INNER, INNER), 1)
        spread = one_hot(
            jnp.logical_and(i == 6 + (j // CELL) * ROWS + j % CELL, j % CELL < ROWS)
        )

        def step(s, carry):
            wp[pl.ds(pl.multiple_of(s * INNER, INNER), INNER), :] = dot(
                spread, wraw[s]
            ).astype(BF16)
            return carry

        lax.fori_loop(0, SIDE, step, 0)

    def gather_one(t, c):
        return [
            remote(
                pieces.at[t, c, m], pieces.at[t, c, m],
                g1_s.at[t, c, j], g1_r.at[t, c, j], group_to[j],
            )
            for j in GORDER
        ]

    def gather_two(t, c):
        return [
            remote(
                cvals.at[t, c, m], cvals.at[t, c, m],
                g2_s.at[t, c, j], g2_r.at[t, c, j], group_to[j],
            )
            for j in GORDER
        ]

    def restrict(t, c):
        ls = pl.ds(c * width, width)
        local = loc[:, :, :, ls].reshape(EXT * PADSLAB, width)
        projected = dot(bt[...], local)
        keep = iota((KMAX, width), 0) < own_count
        pieces[t, c, m] = jnp.where(keep, projected, 0.0).astype(BF16)

    def fine_product(c):
        ls = pl.ds(c * width, width)
        i, j = iota((SLAB, PADSLAB), 0), iota((SLAB, PADSLAB), 1)
        pack = one_hot(
            jnp.logical_and(i == (j // CELL) * ROWS + j % CELL, j % CELL < ROWS)
        )
        for s in range(EXT):
            locc[s * SLAB:(s + 1) * SLAB, ls] = dot(
                pack, loc[s, :, :, ls].reshape(PADSLAB, width)
            ).astype(BF16)
        fine[:, ls] = dot(wp[...], locc[:, ls])

    def core_copies(t, c):
        return [
            remote(
                cores.at[t, c, h], corer.at[t, c, h],
                core_s.at[t, c, h], core_r.at[t, c, h], core_to,
            )
            for h in range(2)
        ]

    def y_copies(t, c):
        return [
            remote(
                ysend.at[t, c, k], yrecv.at[t, c, k],
                y_s.at[t, c, k], y_r.at[t, c, k], y_to,
            )
            for k in range(NZ)
        ]

    def z_copies(t, c):
        return [
            remote(
                zsend.at[t, c, k], zrecv.at[t, c, k],
                z_s.at[t, c, k], z_r.at[t, c, k], z_to[k],
            )
            for k in range(NZ)
        ]

    def block(t, c, own, half):
        side = core if own else 1 - core
        return cbuf[side, pl.ds(half * NZ, NZ)].reshape(NZ * SHARE, KGROUP)

    def coarse(t, c):
        coef[:, pl.ds(c * width, width)] = dot(
            place[...], pieces[t, c].reshape(MEMBERS * KMAX, width)
        ).astype(BF16)
        copies = core_copies(t, c)

        def product(own, half):
            return dot(block(t, c, own, half), coef[:, pl.ds(c * width, width)]).reshape(
                NZ, SHARE, width
            )

        cores[t, c, 0] = product(False, 1 - ylo).astype(BF16)
        copies[0].start()
        pb[c, 0] = product(True, 1 - ylo)
        cores[t, c, 1] = product(False, ylo).astype(BF16)
        copies[1].start()

    def reduce_core(t, c):
        copies, ys = core_copies(t, c), y_copies(t, c)
        copies[0].wait_recv()
        for k in ZORDER:
            zz = lax.rem(z + k, NZ)
            ysend[t, c, k] = (pb[c, 0, zz] + corer[t, c, 0, zz].astype(F32)).astype(BF16)
            ys[k].start()
        pb[c, 1] = dot(block(t, c, True, ylo), coef[:, pl.ds(c * width, width)]).reshape(
            NZ, SHARE, width
        )

    def reduce_y(t, c):
        copies, ys, zs = core_copies(t, c), y_copies(t, c), z_copies(t, c)
        copies[1].wait_recv()
        for k in ZORDER:
            zz = lax.rem(z + k, NZ)
            ys[k].wait_recv()
            value = pb[c, 1, zz] + corer[t, c, 1, zz].astype(F32) + yrecv[t, c, k].astype(F32)
            if k == 0:
                pb[c, 0, 0] = value
            else:
                zsend[t, c, k] = value.astype(BF16)
                zs[k].start()

    def reduce_z(t, c):
        zs = z_copies(t, c)
        total = pb[c, 0, 0]
        for k in ZORDER[::-1]:
            if k:
                zs[k].wait_recv()
                total = total + zrecv[t, c, k].astype(F32)
        cvals[t, c, m] = total.astype(BF16)

    def correct(t, c):
        ls = pl.ds(c * width, width)
        chosen = dot(pick[...], cvals[t, c].reshape(MEMBERS * SHARE, width)).astype(BF16)
        for s in range(SIDE):
            rows = slice(s * INNER, (s + 1) * INNER)
            total = fine[rows, ls] + dot(bint[rows, :], chosen)
            total = total.reshape(SIDE, CELL, width)
            if t == 0:
                sol[s, :, :, ls] = uext[s + 1, 1:1 + SIDE, :, ls] + total
                uext[s + 1, 1:1 + SIDE, :, ls] = total
            else:
                sol[s, :, :, ls] = sol[s, :, :, ls] + total
                for q in range(SIDE):
                    for lane, _ in lane_tiles(c):
                        for comp_id in range(3):
                            out[s, q, :, comp_id, pl.ds(lane, 128)] = sol[
                                s, q, pl.ds(comp_id * 10, 10), pl.ds(lane, 128)
                            ]

    def start_all(copies):
        for copy in copies:
            copy.start()

    def recv_all(copies):
        for copy in copies:
            copy.wait_recv()

    def scoped(name, func, *args):
        with jax.named_scope(name):
            func(*args)

    chunks = range(nch)
    scoped("load0", loads[0].wait)
    scoped("load0", loads[1].wait)
    scoped("unpack", unpack_inputs)
    for c in chunks:
        scoped("stencil", stencil, 0, c)
    scoped("barrier", pl.semaphore_wait, barrier, len(partners))
    for c in chunks:
        for part in range(2):
            scoped("halo_send", start_all, halo_copies(0, c, part, (2, 3, 0, 1)))
    for t in range(SWEEPS):
        if t == 0:
            scoped("tables", tables)
            scoped("load1", loads[2].wait)
            scoped("basis", expand_basis)
        def residual_part(c):
            scoped("end_wait", recv_all, halo_copies(t, c, 0, (2, 3)))
            scoped("end_send", start_all, corner_copies(t, c))

        def restrict_part(c):
            for part in range(2):
                scoped("halo_s", recv_all, halo_copies(t, c, part, (0, 1)))
            scoped("halo_q", recv_all, halo_copies(t, c, 1, (2, 3)))
            scoped("corner", recv_all, corner_copies(t, c))
            scoped("finish", finish_residual, t, c)
            scoped("restrict", restrict, t, c)
            scoped("g1_send", start_all, gather_one(t, c))

        def coarse_part(c):
            scoped("g1_wait", recv_all, gather_one(t, c))
            scoped("coarse", coarse, t, c)

        residual_part(0)
        restrict_part(0)
        residual_part(1)
        if t == 0:
            for copy in loads[3:]:
                scoped("load2", copy.wait)
            scoped("inverse", expand_inverse)
        restrict_part(1)
        scoped("fine", fine_product, 0)
        coarse_part(0)
        scoped("core", reduce_core, t, 0)
        coarse_part(1)
        scoped("core", reduce_core, t, 1)
        scoped("y0", reduce_y, t, 0)
        scoped("fine", fine_product, 1)
        scoped("y1", reduce_y, t, 1)
        for c in chunks:
            scoped("zwait", reduce_z, t, c)
            scoped("g2_send", start_all, gather_two(t, c))
        for c in chunks:
            scoped("g2_wait", recv_all, gather_two(t, c))
            scoped("correct", correct, t, c)
            if t == 0:
                scoped("stencil", stencil, 1, c)
                for part in range(2):
                    scoped("halo_send", start_all, halo_copies(1, c, part, (2, 3, 0, 1)))
    for t in range(SWEEPS):
        for c in chunks:
            for copy in (
                halo_copies(t, c, 0, range(4)) + halo_copies(t, c, 1, range(4))
                + corner_copies(t, c)
                + gather_one(t, c) + core_copies(t, c)
                + y_copies(t, c) + z_copies(t, c)[1:] + gather_two(t, c)
            ):
                copy.wait_send()


def shards(nch, rhs, start, stiffness, sub_inverse, basis, coarse_inverse, offsets):
    def held(array):
        return pltpu.with_memory_space_constraint(array, pltpu.HBM)

    def turned(field):
        return jnp.transpose(field, (0, 1, 3, 2, 4))

    width = LANES // nch
    lead = (SWEEPS, nch)
    vmem = pl.BlockSpec(memory_space=pltpu.VMEM)
    hbm = pl.BlockSpec(memory_space=pl.ANY)
    dma = pltpu.SemaphoreType.DMA
    out = pl.pallas_call(
        functools.partial(kernel, nch),
        name="schwarz",
        out_shape=jax.ShapeDtypeStruct((SIDE, SIDE, 10, 3, LANES), F32),
        in_specs=[pl.BlockSpec(memory_space=pltpu.SMEM), hbm, hbm, vmem, hbm, hbm, hbm],
        out_specs=vmem,
        scratch_shapes=[
            pltpu.VMEM((SIDE, SIDE, 10, 3, LANES), F32),
            pltpu.VMEM((SIDE, SIDE, 10, 3, LANES), F32),
            pltpu.VMEM((SIDE, SIDE, CELL, 128), F32),
            pltpu.VMEM((SIDE, SIDE, CELL, LANES), F32),
            pltpu.VMEM((EXT, EXT, CELL, LANES), F32),
            pltpu.VMEM((SIDE, SIDE, CELL, LANES), F32),
            pltpu.VMEM((EXT, EXT, CELL, LANES), BF16),
            pltpu.VMEM((NLOC, LANES), BF16),
            pltpu.VMEM((SIDE, INNER, NLOC), BF16),
            pltpu.VMEM((SIDE * INNER, NLOC), BF16),
            pltpu.VMEM((NLOC, KMAX), BF16),
            pltpu.VMEM((SIDE * INNER, KMAX), BF16),
            pltpu.VMEM((KMAX, EXT * PADSLAB), BF16),
            pltpu.VMEM((2, 2 * NZ, SHARE, KGROUP), BF16),
            pltpu.VMEM((KGROUP, LANES), BF16),
            pltpu.VMEM((KGROUP, MEMBERS * KMAX), BF16),
            pltpu.VMEM((KMAX, KGROUP), BF16),
            pltpu.VMEM((SIDE * INNER, LANES), F32),
            pltpu.VMEM((nch, 2, NZ, SHARE, width), F32),
            pltpu.VMEM(lead + (4, 2, SIDE, CELL, width), BF16),
            pltpu.VMEM(lead + (4, 2, SIDE, CELL, width), BF16),
            pltpu.VMEM(lead + (4, 2, CELL, width), BF16),
            pltpu.VMEM(lead + (MEMBERS, KMAX, width), BF16),
            pltpu.VMEM(lead + (2, NZ, SHARE, width), BF16),
            pltpu.VMEM(lead + (2, NZ, SHARE, width), BF16),
            pltpu.VMEM(lead + (NZ, SHARE, width), BF16),
            pltpu.VMEM(lead + (NZ, SHARE, width), BF16),
            pltpu.VMEM(lead + (NZ, SHARE, width), BF16),
            pltpu.VMEM(lead + (NZ, SHARE, width), BF16),
            pltpu.VMEM(lead + (MEMBERS, SHARE, width), BF16),
            dma((5 + SIDE,)),
            dma(lead + (2, 4)), dma(lead + (2, 4)),
            dma(lead + (4,)), dma(lead + (4,)),
            dma(lead + (8,)), dma(lead + (8,)),
            dma(lead + (2,)), dma(lead + (2,)),
            dma(lead + (8,)), dma(lead + (8,)),
            dma(lead + (8,)), dma(lead + (8,)),
            dma(lead + (8,)), dma(lead + (8,)),
        ],
        compiler_params=pltpu.CompilerParams(
            collective_id=0, has_side_effects=True, vmem_limit_bytes=44 * 1024 * 1024
        ),
    )(
        held(offsets[0]),
        held(turned(start)),
        held(turned(rhs)),
        held(stiffness),
        held(sub_inverse[0]),
        held(basis[0]),
        held(coarse_inverse.reshape(2 * NZ, 2, SHARE, KGROUP)),
    )
    return turned(out)


def solution(mesh):
    return jax.shard_map(
        functools.partial(shards, 2),
        mesh=mesh,
        in_specs=(
            P("sub", ("crow", "ccol"), None, None, None),
            P("sub", ("crow", "ccol"), None, None, None),
            P("sub", ("crow", "ccol"), None, None),
            P(("sub", "crow", "ccol"), None, None),
            P(("sub", "crow", "ccol"), None, None),
            P(None, ("crow", "ccol"), "sub"),
            P("sub", None),
        ),
        out_specs=P("sub", ("crow", "ccol"), None, None, None),
        check_vma=False,
    )
```
